32 devices in a mesh: groups: 2 (over y), phi: 4 (over z), ev: 4 (over x, core).
Axes of the slice: x: 2, y: 2, z: 4, core: 2. Of those that a mesh axis runs over, the one named last changes fastest.
Arguments:
- cell_feats: bfloat16 [8, 1024, 256], P(('groups', 'ev'), 'phi'), parts along dimension 0, may hold values from -3 to 3
- neighbours: int32 [8, 8, 4], P(('groups', 'ev'), 'phi'), parts along dimension 0, may hold values from 0 to 3
- member_cell: int32 [8, 512], P(('groups', 'ev'), 'phi'), parts along dimension 0, may hold values from 0 to 255, as said below
- member_jet: int32 [8, 512, 1], P(('groups', 'ev'), 'phi'), parts along dimension 0, may hold values from 0 to 15, as said below
- cotangent: bfloat16 [8, 1024, 256], P(('groups', 'ev'), 'phi'), parts along dimension 0, may hold values from -3 to 3
- message_weight: bfloat16 [256, 256], replicated, may hold values from -0.375 to 0.375
- query_weight: bfloat16 [256, 256], replicated, may hold values from -4 to 4
- key_weight: bfloat16 [256, 256], replicated, may hold values from -4 to 4
- value_weight: bfloat16 [256, 256], replicated, may hold values from -0.375 to 0.375
- output_weight: bfloat16 [256, 256], replicated, may hold values from -0.375 to 0.375
Outputs:
- out_cells: bfloat16 [8, 1024, 256], P(('groups', 'ev'), 'phi'), parts along dimension 0
- grad_cells: bfloat16 [8, 1024, 256], P(('groups', 'ev'), 'phi'), parts along dimension 0
- grad_message: float32 [512, 256], P('groups'), parts along dimension 0
- grad_query: float32 [512, 256], P('groups'), parts along dimension 0
- grad_key: float32 [512, 256], P('groups'), parts along dimension 0
- grad_value: float32 [512, 256], P('groups'), parts along dimension 0
- grad_output: float32 [512, 256], P('groups'), parts along dimension 0
The draws below stay inside these ranges and needn't reach their ends.
There are 2 independent parts, one for each index of `groups`. The reference program is written for one: setup_inputs(seed, part) draws one part's arguments, and reference() takes and returns one part's arrays. A program takes and returns all parts, laid end to end along the dimension named above; an argument that names none is the same for every part. Nothing has to cross between parts.
Inputs may be any that keep to these rules, and one draw needn't show every extreme that they name: `member_cell`: within one sector's 128 constituents of an event the cells are distinct. `member_jet`: A constituent of sector p belongs to a jet owned by one of the sectors p - 1 to p + 1 on the loop (jet j is owned by sector j // 4). Among one sector's 128 constituents of an event at most 21 belong to one jet, and some jet has exactly 21 of them.
All inputs are finite; a program needn't handle non-finite values.
Results may differ from the reference program's by a relative error of at most 0.0065.
The reference program's roundings to bfloat16 on the way count: a program that leaves them out, or rounds other values in their place, can miss the bound.
Values may be sent and summed in bfloat16 or wider, within the bound.
No kernel may reach another device: no remote copies, remote signals or barrier semaphores. Data moves between devices by JAX's collectives and lax.ppermute only.
A program may use at most 64 MiB of HBM per device.

```python
import math
import jax
import jax.numpy as jnp
from jax import lax

WIDTH = 256
HEADS = 8
BLOCK = 128
NBRS = 4
JET_DEV = 4
CELLS_DEV = 256
BLOCKS_DEV = 2
CONS_DEV = 128
REACH = 1
WINDOW = 3
CAP = 21
CELLS = 1024
CONS = 512
EVENTS = 4
N_PHI = 4


def draw_member_cell(key, part):
    count = EVENTS * (CONS // CONS_DEV)
    keys = jax.random.split(jax.random.fold_in(key, 11), count)
    picks = jax.vmap(lambda single: jax.random.permutation(single, CELLS_DEV)[:CONS_DEV])(keys)
    return picks.reshape(EVENTS, CONS).astype(jnp.int32)


def draw_member_jet(key, part):
    sectors = CONS // CONS_DEV
    total = WINDOW * JET_DEV * CAP
    heaviness = jax.random.randint(jax.random.fold_in(key, 31), (EVENTS, sectors * JET_DEV), 1, 5)
    base_key = jax.random.fold_in(key, 37)

    def one_sector(flat_index):
        event_index = flat_index // sectors
        sector = flat_index % sectors
        single = jax.random.fold_in(base_key, flat_index)
        first, second, third = jax.random.split(single, 3)
        slot = jnp.arange(total, dtype=jnp.int32)
        local = slot // CAP
        level = slot % CAP
        owner = (sector + local // JET_DEV - REACH + sectors) % sectors
        jet = owner * JET_DEV + local % JET_DEV
        weight = jnp.take(heaviness[event_index], jet)
        chosen = jax.random.randint(first, (), 0, WINDOW * JET_DEV)
        order_key = jax.random.permutation(second, total).astype(jnp.int32)
        score = jnp.where(local == chosen, order_key - total, level * 4 // weight * total + order_key)
        order = jnp.argsort(score, stable=True)[:CONS_DEV]
        picked = jet[order]
        shuffle = jax.random.permutation(third, CONS_DEV)
        return picked[shuffle]
    flat = jax.vmap(one_sector)(jnp.arange(EVENTS * sectors, dtype=jnp.int32))
    return flat.reshape(EVENTS, CONS, 1).astype(jnp.int32)


def paired_weights(key):
    base_key = jax.random.fold_in(key, 23)
    first, second = jax.random.split(base_key, 2)
    shape = (WIDTH, WIDTH)
    root = WIDTH ** (-0.5)
    query_part = jnp.clip(jax.random.normal(first, shape, jnp.float32), -4.0, 4.0)
    other_part = jnp.clip(jax.random.normal(second, shape, jnp.float32), -4.0, 4.0)
    return (query_part * root, other_part * root)


def draw_query_weight(key, part):
    return paired_weights(key)[0].astype(jnp.bfloat16)


def draw_key_weight(key, part):
    return paired_weights(key)[1].astype(jnp.bfloat16)


def place_ends(drawn, rng, least, high):
    place = [jax.random.randint(jax.random.fold_in(rng, axis), (), 0, length) for axis, length in enumerate(drawn.shape)]
    main_axis = drawn.shape.index(max(drawn.shape))
    neighbour = place[:main_axis] + [(place[main_axis] + 1) % drawn.shape[main_axis]] + place[main_axis + 1:]
    return drawn.at[tuple(place)].set(least).at[tuple(neighbour)].set(high)


def spiked(array, own_key, source, target, blocks, factor):
    owner, partner = [(jnp.arange(array.shape[axis_at]) // (array.shape[axis_at] // blocks)).reshape([-1 if axis == axis_at else 1 for axis in range(array.ndim)]) for axis_at in (source, target)]
    chosen = jax.random.permutation(own_key, blocks)[partner]
    strong = (owner == chosen) | (owner == (partner + blocks // 2) % blocks)
    return jnp.where(strong, factor * array, array)


def shard_levels(rng, dims, shards, smallest, high):
    level, own = 1.0, jax.random.fold_in(rng, 6)
    for axis_at, blocks in shards:
        heights = jnp.exp(jax.random.uniform(jax.random.fold_in(own, axis_at), (blocks,), jnp.float32, smallest / len(shards), high / len(shards)))
        level = level * jnp.repeat(heights, dims[axis_at] // blocks).reshape([-1 if axis == axis_at else 1 for axis in range(len(dims))])
    return level


def centred(rng, extent, deviation, most, cuts=(), held_as=jnp.bfloat16):
    entries = deviation * jax.random.normal(rng, extent, jnp.float32)
    if cuts:
        entries = entries * shard_levels(rng, extent, cuts, -0.22, 0.18)
    return jnp.clip(entries, -most, most).astype(held_as)


def gaussian_with(stream_key, dims, spread, most, pieces, heavy, held_as=jnp.bfloat16):
    array = spread * jax.random.normal(stream_key, dims, jnp.float32)
    if pieces:
        array = array * shard_levels(stream_key, dims, pieces, -0.22, 0.18)
    return jnp.clip(spiked(array, jax.random.fold_in(stream_key, 3), *heavy), -most, most).astype(held_as)


def setup_inputs(seed: int = 0, part: int = 0) -> dict:
    key_list = jax.random.split(jax.random.key(seed), 11)
    part_keys = jax.random.split(jax.random.fold_in(key_list[10], part), 11)
    return {
        "cell_feats": centred(part_keys[0], (EVENTS, CELLS, WIDTH), 0.5, 3.0, ((0, 4), (1, 4))),
        "neighbours": place_ends(jax.random.randint(part_keys[1], (EVENTS, N_PHI * BLOCKS_DEV, NBRS), 0, BLOCKS_DEV + 2), jax.random.fold_in(part_keys[1], 1), 0, (BLOCKS_DEV + 2) - 1).astype(jnp.int32),
        "member_cell": draw_member_cell(jax.random.fold_in(jax.random.fold_in(key_list[10], part), 71), part),
        "member_jet": draw_member_jet(jax.random.fold_in(jax.random.fold_in(key_list[10], part), 71), part),
        "cotangent": gaussian_with(part_keys[4], (EVENTS, CELLS, WIDTH), 0.5, 3.0, ((0, 4), (1, 4)), (1, 2, 4, 2.0)),
        "message_weight": centred(key_list[5], (WIDTH, WIDTH), WIDTH ** -0.5, 0.375),
        "query_weight": draw_query_weight(jax.random.fold_in(key_list[10], 71), part),
        "key_weight": draw_key_weight(jax.random.fold_in(key_list[10], 71), part),
        "value_weight": centred(key_list[8], (WIDTH, WIDTH), WIDTH ** -0.5, 0.375),
        "output_weight": centred(key_list[9], (WIDTH, WIDTH), WIDTH ** -0.5, 0.375),
    }


def silu_slope(values):
    sigmoid = jax.nn.sigmoid(values)
    return sigmoid * (1.0 + values * (1.0 - sigmoid))

def attend_forward(members, present, query_weight, key_weight, value_weight, output_weight):
    jet_count, slot_count, channels = members.shape
    head_size = channels // HEADS
    score_scale = 1.0 / math.sqrt(head_size)
    flat_members = members.reshape(jet_count * slot_count, channels)

    def project(weight):
        result = jnp.dot(flat_members, weight, preferred_element_type=jnp.float32)
        return result.astype(jnp.bfloat16).reshape(jet_count, slot_count, HEADS, head_size)
    queries = project(query_weight)
    keyed = project(key_weight)
    valued = project(value_weight)
    scores = jnp.einsum('jqnd,jknd->jnqk', queries.astype(jnp.float32), keyed.astype(jnp.float32))
    scores = jnp.where(present[:, None, None, :] > 0.5, scores * score_scale, -1e+30)
    largest = lax.optimization_barrier(jnp.max(scores, axis=-1, keepdims=True))
    powers = jnp.exp(scores - largest)
    chances = powers / lax.optimization_barrier(jnp.sum(powers, axis=-1, keepdims=True))
    chances_low = chances.astype(jnp.bfloat16)
    mixture = jnp.einsum('jnqk,jknd->jqnd', chances_low.astype(jnp.float32), valued.astype(jnp.float32))
    mixture = mixture.astype(jnp.bfloat16).reshape(jet_count * slot_count, channels)
    attended = jnp.dot(mixture, output_weight, preferred_element_type=jnp.float32).astype(jnp.bfloat16)
    return (attended.reshape(jet_count, slot_count, channels), (queries, keyed, valued, chances, chances_low, mixture))

def attend_backward(members, saved, upstream, query_weight, key_weight, value_weight, output_weight):
    queries, keyed, valued, chances, chances_low, mixture = saved
    jet_count, slot_count, channels = members.shape
    head_size = channels // HEADS
    score_scale = 1.0 / math.sqrt(head_size)
    flat_members = members.reshape(jet_count * slot_count, channels)
    flat_upstream = upstream.reshape(jet_count * slot_count, channels)
    output_term = jnp.dot(mixture.T, flat_upstream, preferred_element_type=jnp.float32)
    grad_mix = jnp.dot(flat_upstream, output_weight.T, preferred_element_type=jnp.float32)
    grad_mix = grad_mix.astype(jnp.bfloat16).reshape(jet_count, slot_count, HEADS, head_size)
    grad_chances = jnp.einsum('jqnd,jknd->jnqk', grad_mix.astype(jnp.float32), valued.astype(jnp.float32))
    grad_vals = jnp.einsum('jnqk,jqnd->jknd', chances_low.astype(jnp.float32), grad_mix.astype(jnp.float32))
    grad_vals = grad_vals.astype(jnp.bfloat16)
    inner_sum = lax.optimization_barrier(jnp.sum(chances * grad_chances, axis=-1, keepdims=True))
    grad_scores = (chances * (grad_chances - inner_sum) * score_scale).astype(jnp.bfloat16)
    grad_queries = jnp.einsum('jnqk,jknd->jqnd', grad_scores.astype(jnp.float32), keyed.astype(jnp.float32))
    grad_keys = jnp.einsum('jnqk,jqnd->jknd', grad_scores.astype(jnp.float32), queries.astype(jnp.float32))
    flat_queries = grad_queries.astype(jnp.bfloat16).reshape(jet_count * slot_count, channels)
    flat_keys = grad_keys.astype(jnp.bfloat16).reshape(jet_count * slot_count, channels)
    flat_vals = grad_vals.reshape(jet_count * slot_count, channels)
    query_term = jnp.dot(flat_members.T, flat_queries, preferred_element_type=jnp.float32)
    key_term = jnp.dot(flat_members.T, flat_keys, preferred_element_type=jnp.float32)
    value_term = jnp.dot(flat_members.T, flat_vals, preferred_element_type=jnp.float32)
    grad_members = jnp.dot(flat_queries, query_weight.T, preferred_element_type=jnp.float32)
    grad_members = grad_members + jnp.dot(flat_keys, key_weight.T, preferred_element_type=jnp.float32)
    grad_members = grad_members + jnp.dot(flat_vals, value_weight.T, preferred_element_type=jnp.float32)
    grad_members = grad_members.astype(jnp.bfloat16).reshape(jet_count, slot_count, channels)
    return (grad_members, (query_term, key_term, value_term, output_term))

def reference(cell_feats, neighbours, member_cell, member_jet, cotangent, message_weight, query_weight, key_weight, value_weight, output_weight):
    events, total_cells, channels = cell_feats.shape
    sectors = N_PHI
    per_device = total_cells // sectors
    blocks = per_device // BLOCK
    members_dev = member_cell.shape[1] // sectors
    jet_count = JET_DEV * sectors
    tiles = cell_feats.reshape(events, sectors, blocks, BLOCK, channels)
    extended = jnp.concatenate([jnp.roll(tiles[:, :, blocks - 1:], 1, axis=1), tiles, jnp.roll(tiles[:, :, :1], -1, axis=1)], axis=2)
    pattern = neighbours.reshape(events, sectors, blocks, NBRS)
    counts = lax.optimization_barrier(jnp.sum((pattern[..., None] == jnp.arange(blocks + 2, dtype=jnp.int32)).astype(jnp.float32), axis=3))
    gathered = jnp.einsum('epbj,epjch->epbch', counts, extended.astype(jnp.float32)) * (1.0 / NBRS)
    flat_gathered = gathered.astype(jnp.bfloat16).reshape(-1, channels)
    before_act = jnp.dot(flat_gathered, message_weight, preferred_element_type=jnp.float32)
    hidden = (cell_feats.reshape(-1, channels).astype(jnp.float32) + jax.nn.silu(before_act)).astype(jnp.bfloat16)
    hidden = hidden.reshape(events, sectors, per_device, channels)
    local_cells = member_cell.reshape(events, sectors, members_dev)
    jet_ids = member_jet.reshape(events, sectors, members_dev)
    onehot = (jet_ids[..., None] == jnp.arange(jet_count, dtype=jnp.int32)).astype(jnp.int32)
    ranks = lax.optimization_barrier(jnp.sum((jnp.cumsum(onehot, axis=2) - onehot) * onehot, axis=3)).astype(jnp.int32)
    event_index = jnp.arange(events, dtype=jnp.int32)[:, None, None]
    sector_index = jnp.arange(sectors, dtype=jnp.int32)[None, :, None]
    owner = jet_ids // JET_DEV
    offset_slot = ((sector_index - owner + REACH + sectors) % sectors).astype(jnp.int32)
    chosen = jnp.take_along_axis(hidden, local_cells[..., None], axis=2)
    cot_cells = cotangent.reshape(events, sectors, per_device, channels)
    cot_chosen = jnp.take_along_axis(cot_cells, local_cells[..., None], axis=2)
    empty_slots = jnp.zeros((events, jet_count, WINDOW, CAP, channels), jnp.bfloat16)
    slot_rows = empty_slots.at[event_index, jet_ids, offset_slot, ranks].set(chosen)
    slot_grads = empty_slots.at[event_index, jet_ids, offset_slot, ranks].set(cot_chosen)
    slot_mask = jnp.zeros((events, jet_count, WINDOW, CAP), jnp.float32).at[event_index, jet_ids, offset_slot, ranks].set(1.0)
    owners = events * sectors
    slot_count = WINDOW * CAP
    items = (slot_rows.reshape(owners, JET_DEV, slot_count, channels), slot_mask.reshape(owners, JET_DEV, slot_count), slot_grads.reshape(owners, JET_DEV, slot_count, channels))

    def owner_step(carry, item):
        members, present, upstream = item
        attended, saved = attend_forward(members, present, query_weight, key_weight, value_weight, output_weight)
        grad_members, terms = attend_backward(members, saved, upstream, query_weight, key_weight, value_weight, output_weight)
        carry = tuple((old + new for old, new in zip(carry, terms)))
        return (carry, (attended, grad_members))
    zero_grad = jnp.zeros((channels, channels), jnp.float32)
    terms, stacked = lax.scan(owner_step, (zero_grad, zero_grad, zero_grad, zero_grad), items)
    attended_all = stacked[0].reshape(events, jet_count, WINDOW, CAP, channels)
    grads_all = stacked[1].reshape(events, jet_count, WINDOW, CAP, channels)
    attended_rows = attended_all[event_index, jet_ids, offset_slot, ranks]
    grad_rows = grads_all[event_index, jet_ids, offset_slot, ranks]
    zero_cells = jnp.zeros((events, sectors, per_device, channels), jnp.float32)
    placed = zero_cells.at[event_index, sector_index, local_cells].set(attended_rows.astype(jnp.float32))
    placed_grad = zero_cells.at[event_index, sector_index, local_cells].set(grad_rows.astype(jnp.float32))
    out_cells = (hidden.astype(jnp.float32) + placed).astype(jnp.bfloat16).reshape(events, total_cells, channels)
    grad_hidden = cot_cells.astype(jnp.float32) + placed_grad
    grad_before = (grad_hidden.reshape(-1, channels) * silu_slope(before_act)).astype(jnp.bfloat16)
    message_term = jnp.dot(flat_gathered.T, grad_before, preferred_element_type=jnp.float32)
    grad_gathered = jnp.dot(grad_before, message_weight.T, preferred_element_type=jnp.float32).astype(jnp.bfloat16)
    grad_gathered = grad_gathered.reshape(events, sectors, blocks, BLOCK, channels)
    grad_extended = jnp.einsum('epbj,epbch->epjch', counts, grad_gathered.astype(jnp.float32)) * (1.0 / NBRS)
    grad_extended = grad_extended.astype(jnp.bfloat16)
    from_lower = jnp.roll(grad_extended[:, :, blocks + 1:], 1, axis=1).astype(jnp.float32)
    from_upper = jnp.roll(grad_extended[:, :, :1], -1, axis=1).astype(jnp.float32)
    summed = grad_hidden.reshape(events, sectors, blocks, BLOCK, channels) + grad_extended[:, :, 1:blocks + 1].astype(jnp.float32)
    summed = summed.at[:, :, :1].add(from_lower)
    summed = summed.at[:, :, blocks - 1:].add(from_upper)
    grad_cells = summed.astype(jnp.bfloat16).reshape(events, total_cells, channels)
    totals = (message_term,) + tuple(terms)
    squares = jnp.sum(jnp.stack([jnp.sum(matrix * matrix) for matrix in totals]))
    bound = math.sqrt(5.0) * channels
    factor = bound / jnp.maximum(jnp.sqrt(squares), bound)
    return (out_cells, grad_cells, totals[0] * factor, totals[1] * factor, totals[2] * factor, totals[3] * factor, totals[4] * factor)
```

```python
import math

import jax
import jax.numpy as jnp
from jax import lax
from jax.experimental import pallas as pl
from jax.experimental.pallas import tpu as pltpu
from jax.sharding import PartitionSpec as P

HEADS = 8
BLOCK = 128
NBRS = 4
JET_DEV = 4
LOW = jnp.bfloat16
FULL = jnp.float32
VMEM = pl.BlockSpec(memory_space=pltpu.VMEM)
SMEM = pl.BlockSpec(memory_space=pltpu.SMEM)


def call(body, outs, scalars, arrays, scratch=()):
    return pl.pallas_call(
        body,
        out_shape=[jax.ShapeDtypeStruct(shape, dtype) for shape, dtype in outs],
        in_specs=[SMEM] * len(scalars) + [VMEM] * len(arrays),
        out_specs=[VMEM] * len(outs),
        scratch_shapes=list(scratch),
    )(*scalars, *arrays)


def shifted(block, axis, distance):
    count = lax.axis_size(axis)
    return lax.ppermute(block, axis, [((i - distance) % count, i) for i in range(count)])


def swapped(block, axis, mask):
    return lax.ppermute(block, axis, [(i, i ^ mask) for i in range(lax.axis_size(axis))])


def mm(a, b):
    return lax.dot_general(a, b, (((1,), (0,)), ((), ())), preferred_element_type=FULL)


def mm_nt(a, b):
    return lax.dot_general(a, b, (((1,), (1,)), ((), ())), preferred_element_type=FULL)


def mm_tn(a, b):
    return lax.dot_general(a, b, (((0,), (0,)), ((), ())), preferred_element_type=FULL)


def iota(shape, dim):
    return lax.broadcasted_iota(jnp.int32, shape, dim)


class Plan:
    def __init__(self, sectors, per_device, members_dev, channels):
        self.sectors, self.cells, self.members, self.channels = sectors, per_device, members_dev, channels
        self.blocks = per_device // BLOCK
        self.radius = min(4, (sectors - 1) // 2)
        self.window = 2 * self.radius + 1
        self.cap = max(2, 2 * members_dev // (JET_DEV * self.window))
        self.used = JET_DEV * self.cap
        self.chunk = -(-(self.used + 1) // 16) * 16
        self.slots = -(-self.window * self.cap // 64) * 64
        self.owned = JET_DEV * self.slots


def index_kernel(plan, where_ref, cell_ref, jet_ref, cot_ref, pick_ref, place_ref, *chunk_refs):
    sector = where_ref[0]
    count, members = plan.chunk, plan.members
    jets = jet_ref[...]
    owner = lax.shift_right_logical(jets, 2)
    offset = owner - sector + plan.radius
    offset = jnp.where(offset < 0, offset + plan.sectors, offset)
    offset = jnp.where(offset >= plan.sectors, offset - plan.sectors, offset)
    inner = lax.bitwise_and(jets, 3)
    row = (offset * JET_DEV + inner).astype(FULL)
    rows, cols = iota((members, members), 0), iota((members, members), 1)
    column = jnp.sum(jnp.where(rows == cols, row, 0.0), axis=1, keepdims=True)
    earlier = jnp.where((column == row) & (rows < cols), 1.0, 0.0)
    rank = jnp.sum(earlier, axis=0, keepdims=True)
    target = offset * count + inner * plan.cap + rank.astype(jnp.int32)
    total = plan.window * count
    slot_hot = jnp.where(iota((total, members), 0) == target, 1.0, 0.0).astype(LOW)
    cell_hot = jnp.where(iota((plan.cells, members), 0) == cell_ref[...], 1.0, 0.0).astype(LOW)
    pick = mm_nt(slot_hot, cell_hot).astype(LOW)
    pick_ref[...] = pick
    place_ref[...] = mm_nt(cell_hot, slot_hot).astype(LOW)
    ones = jnp.ones((8, members), LOW)
    wide = iota((plan.channels, members), 0)
    mask_row = iota((count, plan.channels), 0) == plan.used
    chosen = mm(pick, cot_ref[...])
    for w in range(plan.window):
        hot = jnp.where((wide + w * count == target) & (wide < count), 1.0, 0.0).astype(LOW)
        present = mm_nt(ones, hot)[0:1, :]
        part = chosen[w * count : (w + 1) * count, :]
        chunk_refs[w][...] = jnp.where(mask_row, present, part).astype(LOW)


def hidden_kernel(plan, nbr_ref, cell_ref, low_ref, high_ref, weight_ref, pick_ref, gathered_ref, before_ref, hidden_ref, *chunk_refs):
    blocks = plan.blocks
    entries = [low_ref[...].astype(FULL)]
    entries += [cell_ref[b * BLOCK : (b + 1) * BLOCK, :].astype(FULL) for b in range(blocks)]
    entries += [high_ref[...].astype(FULL)]
    for b in range(blocks):
        total = None
        for j, entry in enumerate(entries):
            times = sum((nbr_ref[b, k] == j).astype(FULL) for k in range(NBRS)) * (1.0 / NBRS)
            total = entry * times if total is None else total + entry * times
        gathered_ref[b * BLOCK : (b + 1) * BLOCK, :] = total.astype(LOW)
    before = mm(gathered_ref[...], weight_ref[...])
    before_ref[...] = before
    silu = before * (1.0 / (1.0 + jnp.exp(-before)))
    hidden = (cell_ref[...].astype(FULL) + silu).astype(LOW)
    hidden_ref[...] = hidden
    chosen = mm(pick_ref[...], hidden).astype(LOW)
    for w in range(plan.window):
        chunk_refs[w][...] = chosen[w * plan.chunk : (w + 1) * plan.chunk, :]


def attend_kernel(plan, *refs):
    window, count, slots, owned, channels = plan.window, plan.chunk, plan.slots, plan.owned, plan.channels
    feat_refs, cot_refs = refs[:window], refs[window : 2 * window]
    wq_ref, wk_ref, wv_ref, wo_ref = refs[2 * window : 2 * window + 4]
    back_refs = refs[2 * window + 4 : 3 * window + 4]
    term_ref, parts_ref = refs[3 * window + 4 :]
    head = channels // HEADS
    scale = 1.0 / math.sqrt(head)

    def seat(c, w):
        jet = sum((c >= t * plan.cap).astype(jnp.int32) for t in range(1, JET_DEV))
        return jnp.where(c < plan.used, c + jet * (slots - plan.cap) + w * plan.cap, -1)

    members = upstream = present = None
    base = plan.used // 16 * 16
    for w in range(window):
        hot = jnp.where(iota((owned, count), 0) == seat(iota((owned, count), 1), w), 1.0, 0.0)
        low = hot.astype(LOW)
        m, u = mm(low, feat_refs[w][...]), mm(low, cot_refs[w][...])
        tail = cot_refs[w][base : base + 16, :].astype(FULL)
        row = jnp.sum(jnp.where(iota(tail.shape, 0) == plan.used - base, tail, 0.0), axis=0, keepdims=True)
        p = jnp.sum(hot * row[:, :count], axis=1, keepdims=True)
        members = m if members is None else members + m
        upstream = u if upstream is None else upstream + u
        present = p if present is None else present + p
    members, upstream = members.astype(LOW), upstream.astype(LOW)
    queries = mm(members, wq_ref[...]).astype(LOW)
    keys = mm(members, wk_ref[...]).astype(LOW)
    vals = mm(members, wv_ref[...]).astype(LOW)
    grad_mix = mm_nt(upstream, wo_ref[...]).astype(LOW)
    lane = iota((1, channels), 1)
    head_of = [(lane >= h * head) & (lane < (h + 1) * head) for h in range(HEADS)]
    low_of = [jnp.where(h, 1.0, 0.0).astype(LOW) for h in head_of]

    def spread(block):
        return jnp.concatenate([block * low_of[h] for h in range(HEADS)], axis=0)

    def merged(wide):
        total = None
        for h in range(HEADS):
            part = jnp.where(head_of[h], wide[h * slots : (h + 1) * slots, :], 0.0)
            total = part if total is None else total + part
        return total

    mixture, grad_q, grad_k, grad_v = [], [], [], []
    for j in range(JET_DEV):
        span = slice(j * slots, (j + 1) * slots)
        q, k, v, g = queries[span], keys[span], vals[span], grad_mix[span]
        here = present[span] > 0.5
        q_wide, g_wide = spread(q), spread(g)
        scores = jnp.where(here, mm_nt(k, q_wide) * scale, -1e30)
        powers = jnp.exp(scores - jnp.max(scores, axis=0, keepdims=True))
        chances = powers * (1.0 / jnp.sum(powers, axis=0, keepdims=True))
        chances_low = chances.astype(LOW)
        grad_chances = mm_nt(v, g_wide)
        inner = jnp.sum(chances * grad_chances, axis=0, keepdims=True)
        grad_scores = (chances * (grad_chances - inner) * scale).astype(LOW)
        mixture.append(merged(mm_tn(chances_low, v)).astype(LOW))
        grad_q.append(merged(mm_tn(grad_scores, k)).astype(LOW))
        grad_k.append(mm(grad_scores, q_wide).astype(LOW))
        grad_v.append(mm(chances_low, g_wide).astype(LOW))
    mixture, grad_q, grad_k, grad_v = [jnp.concatenate(x, axis=0) for x in (mixture, grad_q, grad_k, grad_v)]
    attended = mm(mixture, wo_ref[...]).astype(LOW)
    grad_members = mm_nt(grad_q, wq_ref[...]) + mm_nt(grad_k, wk_ref[...]) + mm_nt(grad_v, wv_ref[...])
    grad_members = grad_members.astype(LOW)
    for w in range(window):
        hot = jnp.where(seat(iota((count, owned), 0), w) == iota((count, owned), 1), 1.0, 0.0).astype(LOW)
        back_refs[w][:count, :] = mm(hot, attended).astype(LOW)
        back_refs[w][count:, :] = mm(hot, grad_members).astype(LOW)
    parts_ref[0] = members
    parts_ref[1] = upstream
    parts_ref[2] = mixture
    parts_ref[3] = grad_q
    parts_ref[4] = grad_k
    parts_ref[5] = grad_v
    members_t, mixture_t = members.T, mixture.T
    term_ref[0:channels] = mm(members_t, grad_q)
    term_ref[channels : 2 * channels] = mm(members_t, grad_k)
    term_ref[2 * channels : 3 * channels] = mm(members_t, grad_v)
    term_ref[3 * channels :] = mm(mixture_t, upstream)


def return_kernel(plan, nbr_ref, *refs):
    window, count = plan.window, plan.chunk
    back_refs = refs[:window]
    place_ref, hidden_ref, cot_ref, before_ref, gathered_ref, weight_ref = refs[window : window + 6]
    out_ref, kept_ref, first_ref, last_ref, term_ref, rows_ref = refs[window + 6 :]
    place = place_ref[...]
    for w in range(window):
        rows_ref[0, w * count : (w + 1) * count, :] = back_refs[w][:count, :]
        rows_ref[1, w * count : (w + 1) * count, :] = back_refs[w][count:, :]
    out_ref[...] = (hidden_ref[...].astype(FULL) + mm(place, rows_ref[0])).astype(LOW)
    grad_hidden = cot_ref[...].astype(FULL) + mm(place, rows_ref[1])
    before = before_ref[...]
    sigmoid = 1.0 / (1.0 + jnp.exp(-before))
    slope = sigmoid * (1.0 + before * (1.0 - sigmoid))
    grad_before = (grad_hidden * slope).astype(LOW)
    grad_gathered = mm_nt(grad_before, weight_ref[...]).astype(LOW).astype(FULL)

    def extended(j):
        total = None
        for b in range(plan.blocks):
            times = sum((nbr_ref[b, k] == j).astype(FULL) for k in range(NBRS)) * (1.0 / NBRS)
            part = grad_gathered[b * BLOCK : (b + 1) * BLOCK, :] * times
            total = part if total is None else total + part
        return total.astype(LOW)

    first_ref[...] = extended(0)
    last_ref[...] = extended(plan.blocks + 1)
    for b in range(plan.blocks):
        span = slice(b * BLOCK, (b + 1) * BLOCK)
        kept_ref[span, :] = grad_hidden[span] + extended(b + 1).astype(FULL)
    term_ref[...] = mm_tn(gathered_ref[...], grad_before)


def edges_kernel(plan, kept_ref, low_ref, high_ref, out_ref):
    last = plan.cells - BLOCK
    if last:
        out_ref[:BLOCK, :] = (kept_ref[:BLOCK, :] + low_ref[...].astype(FULL)).astype(LOW)
        if last > BLOCK:
            out_ref[BLOCK:last, :] = kept_ref[BLOCK:last, :].astype(LOW)
        out_ref[last:, :] = (kept_ref[last:, :] + high_ref[...].astype(FULL)).astype(LOW)
    else:
        out_ref[...] = (kept_ref[...] + low_ref[...].astype(FULL) + high_ref[...].astype(FULL)).astype(LOW)


def halve_kernel(kept_ref, came_ref, bit_ref, send_ref, keep_ref, total_ref):
    half = kept_ref.shape[0] // 2
    total_ref[0] = kept_ref[:half, :] + came_ref[:half, :].astype(FULL)
    total_ref[1] = kept_ref[half:, :] + came_ref[half:, :].astype(FULL)
    bit = bit_ref[0]
    keep_ref[...] = total_ref[bit]
    send_ref[...] = total_ref[1 - bit].astype(LOW)


def scale_kernel(channels, total_ref, *out_refs):
    bound = math.sqrt(5.0) * channels
    squares = jnp.zeros((1, 1), FULL)
    for t in range(5):
        part = total_ref[t * channels : (t + 1) * channels, :].astype(FULL)
        squares = squares + jnp.sum(jnp.sum(part * part, axis=0, keepdims=True), axis=1, keepdims=True)
    factor = bound / jnp.maximum(jnp.sqrt(squares), bound)
    for t in range(5):
        out_refs[t][...] = total_ref[t * channels : (t + 1) * channels, :].astype(FULL) * factor


def summed(terms):
    stages = []
    for axis in ("ev", "phi"):
        mask = 1
        while mask < lax.axis_size(axis):
            stages.append((axis, mask))
            mask *= 2
    bits = [(lax.axis_index(axis) & mask) // mask for axis, mask in stages]
    kept = terms
    for (axis, mask), bit in zip(stages, bits):
        half = kept.shape[0] // 2
        away = lax.dynamic_slice_in_dim(kept, (1 - bit) * half, half, 0).astype(LOW)
        kept = lax.dynamic_slice_in_dim(kept, bit * half, half, 0)
        kept = kept + swapped(away, axis, mask).astype(FULL)
    whole = kept.astype(LOW)
    for (axis, mask), bit in zip(reversed(stages), reversed(bits)):
        other = swapped(whole, axis, mask)
        whole = jnp.where(bit == 0, jnp.concatenate([whole, other], 0), jnp.concatenate([other, whole], 0))
    return whole


def on_device(cell_feats, neighbours, member_cell, member_jet, cotangent, message_weight, query_weight, key_weight, value_weight, output_weight):
    events, per_device, channels = cell_feats.shape
    assert events == 1
    members_dev = member_cell.shape[1]
    plan = Plan(lax.axis_size("phi"), per_device, members_dev, channels)
    window, chunk, radius = plan.window, plan.chunk, plan.radius
    place = lax.axis_index("phi").astype(jnp.int32).reshape(1)
    cells, cot, nbrs = cell_feats[0], cotangent[0], neighbours[0]
    low = shifted(cells[per_device - BLOCK :], "phi", 1)
    high = shifted(cells[:BLOCK], "phi", -1)
    total = window * chunk
    pick, put, *cot_chunks = call(
        lambda *refs: index_kernel(plan, *refs),
        [((total, per_device), LOW), ((per_device, total), LOW)] + [((chunk, channels), LOW)] * window,
        [place],
        [member_cell.reshape(1, members_dev), member_jet.reshape(1, members_dev), cot],
    )
    gathered, before, hidden, *chunks = call(
        lambda *refs: hidden_kernel(plan, *refs),
        [((per_device, channels), LOW), ((per_device, channels), FULL), ((per_device, channels), LOW)]
        + [((chunk, channels), LOW)] * window,
        [nbrs],
        [cells, low, high, message_weight, pick],
    )

    def sent(parts, sign):
        return [part if w == radius else shifted(part, "phi", sign * (w - radius)) for w, part in enumerate(parts)]

    feats = sent(chunks, 1)
    cots = sent(cot_chunks, 1)
    *backs, terms, _ = call(
        lambda *refs: attend_kernel(plan, *refs),
        [((2 * chunk, channels), LOW)] * window + [((4 * channels, channels), FULL), ((6, plan.owned, channels), LOW)],
        [],
        [*feats, *cots, query_weight, key_weight, value_weight, output_weight],
    )
    backs = sent(backs, -1)
    out_cells, kept, first, last, message_term = call(
        lambda *refs: return_kernel(plan, *refs),
        [((per_device, channels), LOW), ((per_device, channels), FULL), ((BLOCK, channels), LOW), ((BLOCK, channels), LOW), ((channels, channels), FULL)],
        [nbrs],
        [*backs, put, hidden, cot, before, gathered, message_weight],
        [pltpu.VMEM((2, total, channels), LOW)],
    )
    from_lower = shifted(last, "phi", 1)
    from_upper = shifted(first, "phi", -1)
    (grad_cells,) = call(
        lambda *refs: edges_kernel(plan, *refs), [((per_device, channels), LOW)], [], [kept, from_lower, from_upper]
    )
    whole = summed(jnp.concatenate([message_term, terms], axis=0))
    grads = call(lambda *refs: scale_kernel(channels, *refs), [((channels, channels), FULL)] * 5, [], [whole])
    return (out_cells[None], grad_cells[None], *grads)


def solution(mesh):
    cells = P(("groups", "ev"), "phi", None)
    flat = P(("groups", "ev"), "phi")
    weights = P("groups", None)
    return jax.shard_map(
        on_device,
        mesh=mesh,
        in_specs=(cells, cells, flat, cells, cells, P(), P(), P(), P(), P()),
        out_specs=(cells, cells, weights, weights, weights, weights, weights),
        check_vma=False,
    )
```

```python
import math

import jax
import jax.numpy as jnp
from jax import lax
from jax.experimental import pallas as pl
from jax.experimental.pallas import tpu as pltpu
from jax.sharding import PartitionSpec as P

HEADS = 8
BLOCK = 128
NBRS = 4
JET_DEV = 4
LOW = jnp.bfloat16
FULL = jnp.float32
VMEM = pl.BlockSpec(memory_space=pltpu.VMEM)
SMEM = pl.BlockSpec(memory_space=pltpu.SMEM)


def call(body, outs, scalars, arrays, scratch=(), final=False):
    kind = jax.ShapeDtypeStruct if final else pltpu.VMEM
    return pl.pallas_call(
        body,
        out_shape=[kind(shape, dtype) for shape, dtype in outs],
        in_specs=[SMEM] * len(scalars) + [VMEM] * len(arrays),
        out_specs=[VMEM] * len(outs),
        scratch_shapes=list(scratch),
    )(*scalars, *[pltpu.with_memory_space_constraint(x, pltpu.VMEM) for x in arrays])


def shifted(block, axis, distance):
    count = lax.axis_size(axis)
    return lax.ppermute(block, axis, [((i - distance) % count, i) for i in range(count)])


def swapped(block, axis, mask):
    return lax.ppermute(block, axis, [(i, i ^ mask) for i in range(lax.axis_size(axis))])


def mm(a, b):
    return lax.dot_general(a, b, (((1,), (0,)), ((), ())), preferred_element_type=FULL)


def mm_nt(a, b):
    return lax.dot_general(a, b, (((1,), (1,)), ((), ())), preferred_element_type=FULL)


def mm_tn(a, b):
    return lax.dot_general(a, b, (((0,), (0,)), ((), ())), preferred_element_type=FULL)


def iota(shape, dim):
    return lax.broadcasted_iota(jnp.int32, shape, dim)


class Plan:
    def __init__(self, sectors, per_device, members_dev, channels):
        self.sectors, self.cells, self.members, self.channels = sectors, per_device, members_dev, channels
        self.blocks = per_device // BLOCK
        self.radius = min(4, (sectors - 1) // 2)
        self.window = 2 * self.radius + 1
        self.cap = max(2, 2 * members_dev // (JET_DEV * self.window))
        self.used = JET_DEV * self.cap
        self.chunk = -(-(self.used + 1) // 16) * 16
        self.slots = -(-self.window * self.cap // 64) * 64
        self.owned = JET_DEV * self.slots


def index_kernel(plan, where_ref, cell_ref, jet_ref, cot_ref, pick_ref, place_ref, *chunk_refs):
    sector = where_ref[0]
    count, members = plan.chunk, plan.members
    jets = jet_ref[...]
    owner = lax.shift_right_logical(jets, 2)
    offset = owner - sector + plan.radius
    offset = jnp.where(offset < 0, offset + plan.sectors, offset)
    offset = jnp.where(offset >= plan.sectors, offset - plan.sectors, offset)
    inner = lax.bitwise_and(jets, 3)
    row = (offset * JET_DEV + inner).astype(FULL)
    rows, cols = iota((members, members), 0), iota((members, members), 1)
    column = jnp.sum(jnp.where(rows == cols, row, 0.0), axis=1, keepdims=True)
    earlier = jnp.where((column == row) & (rows < cols), 1.0, 0.0)
    rank = jnp.sum(earlier, axis=0, keepdims=True)
    target = offset * count + inner * plan.cap + rank.astype(jnp.int32)
    total = plan.window * count
    slot_hot = jnp.where(iota((total, members), 0) == target, 1.0, 0.0).astype(LOW)
    cell_hot = jnp.where(iota((plan.cells, members), 0) == cell_ref[...], 1.0, 0.0).astype(LOW)
    pick = mm_nt(slot_hot, cell_hot).astype(LOW)
    pick_ref[...] = pick
    place_ref[...] = mm_nt(cell_hot, slot_hot).astype(LOW)
    ones = jnp.ones((8, members), LOW)
    wide = iota((plan.channels, members), 0)
    mask_row = iota((count, plan.channels), 0) == plan.used
    chosen = mm(pick, cot_ref[...])
    for w in range(plan.window):
        hot = jnp.where((wide + w * count == target) & (wide < count), 1.0, 0.0).astype(LOW)
        present = mm_nt(ones, hot)[0:1, :]
        part = chosen[w * count : (w + 1) * count, :]
        chunk_refs[w][...] = jnp.where(mask_row, present, part).astype(LOW)


def hidden_kernel(plan, nbr_ref, cell_ref, low_ref, high_ref, weight_ref, pick_ref, gathered_ref, before_ref, hidden_ref, *chunk_refs):
    blocks = plan.blocks
    entries = [low_ref[...].astype(FULL)]
    entries += [cell_ref[b * BLOCK : (b + 1) * BLOCK, :].astype(FULL) for b in range(blocks)]
    entries += [high_ref[...].astype(FULL)]
    for b in range(blocks):
        total = None
        for j, entry in enumerate(entries):
            times = sum((nbr_ref[b, k] == j).astype(FULL) for k in range(NBRS)) * (1.0 / NBRS)
            total = entry * times if total is None else total + entry * times
        gathered_ref[b * BLOCK : (b + 1) * BLOCK, :] = total.astype(LOW)
    before = mm(gathered_ref[...], weight_ref[...])
    before_ref[...] = before
    silu = before * (1.0 / (1.0 + jnp.exp(-before)))
    hidden = (cell_ref[...].astype(FULL) + silu).astype(LOW)
    hidden_ref[...] = hidden
    chosen = mm(pick_ref[...], hidden).astype(LOW)
    for w in range(plan.window):
        chunk_refs[w][...] = chosen[w * plan.chunk : (w + 1) * plan.chunk, :]


def attend_kernel(plan, *refs):
    window, count, slots, owned, channels = plan.window, plan.chunk, plan.slots, plan.owned, plan.channels
    feat_refs, cot_refs = refs[:window], refs[window : 2 * window]
    wq_ref, wk_ref, wv_ref, wo_ref = refs[2 * window : 2 * window + 4]
    back_refs = refs[2 * window + 4 : 3 * window + 4]
    (parts_ref,) = refs[3 * window + 4 :]
    head = channels // HEADS
    scale = 1.0 / math.sqrt(head)

    def seat(c, w):
        jet = sum((c >= t * plan.cap).astype(jnp.int32) for t in range(1, JET_DEV))
        return jnp.where(c < plan.used, c + jet * (slots - plan.cap) + w * plan.cap, -1)

    members = upstream = present = None
    base = plan.used // 16 * 16
    for w in range(window):
        hot = jnp.where(iota((owned, count), 0) == seat(iota((owned, count), 1), w), 1.0, 0.0)
        low = hot.astype(LOW)
        m, u = mm(low, feat_refs[w][...]), mm(low, cot_refs[w][...])
        tail = cot_refs[w][base : base + 16, :].astype(FULL)
        row = jnp.sum(jnp.where(iota(tail.shape, 0) == plan.used - base, tail, 0.0), axis=0, keepdims=True)
        p = jnp.sum(hot * row[:, :count], axis=1, keepdims=True)
        members = m if members is None else members + m
        upstream = u if upstream is None else upstream + u
        present = p if present is None else present + p
    members, upstream = members.astype(LOW), upstream.astype(LOW)
    queries = mm(members, wq_ref[...]).astype(LOW)
    keys = mm(members, wk_ref[...]).astype(LOW)
    vals = mm(members, wv_ref[...]).astype(LOW)
    grad_mix = mm_nt(upstream, wo_ref[...]).astype(LOW)
    lane = iota((1, channels), 1)
    head_of = [(lane >= h * head) & (lane < (h + 1) * head) for h in range(HEADS)]
    low_of = [jnp.where(h, 1.0, 0.0).astype(LOW) for h in head_of]

    def spread(block):
        return jnp.concatenate([block * low_of[h] for h in range(HEADS)], axis=0)

    def merged(wide):
        total = None
        for h in range(HEADS):
            part = jnp.where(head_of[h], wide[h * slots : (h + 1) * slots, :], 0.0)
            total = part if total is None else total + part
        return total

    mixture, grad_q, grad_k, grad_v = [], [], [], []
    for j in range(JET_DEV):
        span = slice(j * slots, (j + 1) * slots)
        q, k, v, g = queries[span], keys[span], vals[span], grad_mix[span]
        here = present[span] > 0.5
        q_wide, g_wide = spread(q), spread(g)
        scores = jnp.where(here, mm_nt(k, q_wide) * scale, -1e30)
        powers = jnp.exp(scores - jnp.max(scores, axis=0, keepdims=True))
        chances = powers * (1.0 / jnp.sum(powers, axis=0, keepdims=True))
        chances_low = chances.astype(LOW)
        grad_chances = mm_nt(v, g_wide)
        inner = jnp.sum(chances * grad_chances, axis=0, keepdims=True)
        grad_scores = (chances * (grad_chances - inner) * scale).astype(LOW)
        mixture.append(merged(mm_tn(chances_low, v)).astype(LOW))
        grad_q.append(merged(mm_tn(grad_scores, k)).astype(LOW))
        grad_k.append(mm(grad_scores, q_wide).astype(LOW))
        grad_v.append(mm(chances_low, g_wide).astype(LOW))
    mixture, grad_q, grad_k, grad_v = [jnp.concatenate(x, axis=0) for x in (mixture, grad_q, grad_k, grad_v)]
    attended = mm(mixture, wo_ref[...]).astype(LOW)
    grad_members = mm_nt(grad_q, wq_ref[...]) + mm_nt(grad_k, wk_ref[...]) + mm_nt(grad_v, wv_ref[...])
    grad_members = grad_members.astype(LOW)
    for w in range(window):
        hot = jnp.where(seat(iota((count, owned), 0), w) == iota((count, owned), 1), 1.0, 0.0).astype(LOW)
        back_refs[w][:count, :] = mm(hot, attended).astype(LOW)
        back_refs[w][count:, :] = mm(hot, grad_members).astype(LOW)
    parts_ref[0] = members
    parts_ref[1] = upstream
    parts_ref[2] = mixture
    parts_ref[3] = grad_q
    parts_ref[4] = grad_k
    parts_ref[5] = grad_v


def term_kernel(channels, bit_ref, parts_ref, send_ref, keep_ref):
    bit = bit_ref[0]
    for half, ref in ((1 - bit, send_ref), (bit, keep_ref)):
        for t in range(2):
            term = 2 * half + t
            left = parts_ref[jnp.where(term == 3, 2, 0)]
            right = parts_ref[jnp.where(term == 3, 1, 3 + term)]
            ref[t * channels : (t + 1) * channels, :] = mm_tn(left, right).astype(ref.dtype)


def return_kernel(plan, nbr_ref, bit_ref, *refs):
    window, count = plan.window, plan.chunk
    back_refs = refs[:window]
    place_ref, hidden_ref, cot_ref, before_ref, gathered_ref, weight_ref = refs[window : window + 6]
    out_ref, kept_ref, first_ref, last_ref, send_ref, keep_ref, rows_ref, term_ref = refs[window + 6 :]
    place = place_ref[...]
    for w in range(window):
        rows_ref[0, w * count : (w + 1) * count, :] = back_refs[w][:count, :]
        rows_ref[1, w * count : (w + 1) * count, :] = back_refs[w][count:, :]
    out_ref[...] = (hidden_ref[...].astype(FULL) + mm(place, rows_ref[0])).astype(LOW)
    grad_hidden = cot_ref[...].astype(FULL) + mm(place, rows_ref[1])
    before = before_ref[...]
    sigmoid = 1.0 / (1.0 + jnp.exp(-before))
    slope = sigmoid * (1.0 + before * (1.0 - sigmoid))
    grad_before = (grad_hidden * slope).astype(LOW)
    grad_gathered = mm_nt(grad_before, weight_ref[...]).astype(LOW).astype(FULL)

    def extended(j):
        total = None
        for b in range(plan.blocks):
            times = sum((nbr_ref[b, k] == j).astype(FULL) for k in range(NBRS)) * (1.0 / NBRS)
            part = grad_gathered[b * BLOCK : (b + 1) * BLOCK, :] * times
            total = part if total is None else total + part
        return total.astype(LOW)

    first_ref[...] = extended(0)
    last_ref[...] = extended(plan.blocks + 1)
    for b in range(plan.blocks):
        span = slice(b * BLOCK, (b + 1) * BLOCK)
        kept_ref[span, :] = grad_hidden[span] + extended(b + 1).astype(FULL)
    half = plan.channels // 2
    term_ref[...] = mm_tn(gathered_ref[...], grad_before).reshape(2, half, plan.channels)
    send_ref[...] = term_ref[1 - bit_ref[0]].astype(LOW)
    keep_ref[...] = term_ref[bit_ref[0]]


def edges_kernel(plan, kept_ref, low_ref, high_ref, out_ref):
    last = plan.cells - BLOCK
    if last:
        out_ref[:BLOCK, :] = (kept_ref[:BLOCK, :] + low_ref[...].astype(FULL)).astype(LOW)
        if last > BLOCK:
            out_ref[BLOCK:last, :] = kept_ref[BLOCK:last, :].astype(LOW)
        out_ref[last:, :] = (kept_ref[last:, :] + high_ref[...].astype(FULL)).astype(LOW)
    else:
        out_ref[...] = (kept_ref[...] + low_ref[...].astype(FULL) + high_ref[...].astype(FULL)).astype(LOW)


def rows_of(ref, at, count):
    return ref[pl.ds(pl.multiple_of(at * count, count), count), :]


def halve_kernel(bit_ref, kept_ref, came_ref, send_ref, keep_ref):
    half = kept_ref.shape[0] // 2
    bit = bit_ref[0]
    keep_ref[...] = rows_of(kept_ref, bit, half) + rows_of(came_ref, bit, half).astype(FULL)
    send_ref[...] = (rows_of(kept_ref, 1 - bit, half) + rows_of(came_ref, 1 - bit, half).astype(FULL)).astype(LOW)


def quarter_kernel(place_ref, kept_ref, came_ref, keep_ref, *send_refs):
    size = kept_ref.shape[0] // 4
    for mask in range(4):
        at = lax.bitwise_xor(place_ref[0], mask)
        part = rows_of(kept_ref, at, size) + rows_of(came_ref, at, size).astype(FULL)
        if mask:
            send_refs[mask - 1][...] = part.astype(LOW)
        else:
            keep_ref[...] = part


def add_kernel(*refs):
    total = refs[0][...].astype(FULL)
    for ref in refs[1:-1]:
        total = total + ref[...].astype(FULL)
    refs[-1][...] = total.astype(LOW)


def join_kernel(place_ref, *refs):
    out_ref = refs[-1]
    size = refs[0].shape[0]
    for mask, ref in enumerate(refs[:-1]):
        at = lax.bitwise_xor(place_ref[0], mask)
        out_ref[pl.ds(pl.multiple_of(at * size, size), size), :] = ref[...]


def joined_kernel(bit_ref, own_ref, came_ref, term_a_ref, term_b_ref, out_ref):
    size = own_ref.shape[0]
    bit = bit_ref[0]
    out_ref[pl.ds(pl.multiple_of(bit * size, size), size), :] = own_ref[...]
    out_ref[pl.ds(pl.multiple_of((1 - bit) * size, size), size), :] = came_ref[...]
    out_ref[2 * size :, :] = (term_a_ref[...].astype(FULL) + term_b_ref[...].astype(FULL)).astype(LOW)


def total_of(squares_of):
    return jnp.sum(jnp.sum(squares_of * squares_of, axis=0, keepdims=True), axis=1, keepdims=True)


def scale_kernel(channels, bit_ref, own_ref, came_ref, *refs):
    out_refs, both_ref = refs[:5], refs[5]
    bound = math.sqrt(5.0) * channels
    squares = total_of(own_ref[...].astype(FULL)) + total_of(came_ref[...].astype(FULL))
    factor = bound / jnp.maximum(jnp.sqrt(squares), bound)
    both_ref[bit_ref[0]] = own_ref[...]
    both_ref[1 - bit_ref[0]] = came_ref[...]
    half = channels // 2
    for h in range(2):
        for t in range(2):
            out_refs[1 + 2 * h + t][...] = both_ref[h, t * channels : (t + 1) * channels, :].astype(FULL) * factor
        out_refs[0][h * half : (h + 1) * half, :] = both_ref[h, 2 * channels :, :].astype(FULL) * factor


def summed(terms):
    stages = []
    for axis in ("ev", "phi"):
        mask = 1
        while mask < lax.axis_size(axis):
            stages.append((axis, mask))
            mask *= 2
    bits = [(lax.axis_index(axis) & mask) // mask for axis, mask in stages]
    kept = terms
    for (axis, mask), bit in zip(stages, bits):
        half = kept.shape[0] // 2
        away = lax.dynamic_slice_in_dim(kept, (1 - bit) * half, half, 0).astype(LOW)
        kept = lax.dynamic_slice_in_dim(kept, bit * half, half, 0)
        kept = kept + swapped(away, axis, mask).astype(FULL)
    whole = kept.astype(LOW)
    for (axis, mask), bit in zip(reversed(stages), reversed(bits)):
        other = swapped(whole, axis, mask)
        whole = jnp.where(bit == 0, jnp.concatenate([whole, other], 0), jnp.concatenate([other, whole], 0))
    return whole


def on_device(cell_feats, neighbours, member_cell, member_jet, cotangent, message_weight, query_weight, key_weight, value_weight, output_weight):
    events, per_device, channels = cell_feats.shape
    assert events == 1
    members_dev = member_cell.shape[1]
    plan = Plan(lax.axis_size("phi"), per_device, members_dev, channels)
    window, chunk, radius = plan.window, plan.chunk, plan.radius
    place = lax.axis_index("phi").astype(jnp.int32).reshape(1)
    cells, cot, nbrs = cell_feats[0], cotangent[0], neighbours[0]
    low = shifted(cells[per_device - BLOCK :], "phi", 1)
    high = shifted(cells[:BLOCK], "phi", -1)
    total = window * chunk
    pick, put, *cot_chunks = call(
        lambda *refs: index_kernel(plan, *refs),
        [((total, per_device), LOW), ((per_device, total), LOW)] + [((chunk, channels), LOW)] * window,
        [place],
        [member_cell.reshape(1, members_dev), member_jet.reshape(1, members_dev), cot],
    )
    gathered, before, hidden, *chunks = call(
        lambda *refs: hidden_kernel(plan, *refs),
        [((per_device, channels), LOW), ((per_device, channels), FULL), ((per_device, channels), LOW)]
        + [((chunk, channels), LOW)] * window,
        [nbrs],
        [cells, low, high, message_weight, pick],
    )

    def sent(parts, sign):
        return [part if w == radius else shifted(part, "phi", sign * (w - radius)) for w, part in enumerate(parts)]

    feats = sent(chunks, 1)
    cots = sent(cot_chunks, 1)
    *backs, parts = call(
        lambda *refs: attend_kernel(plan, *refs),
        [((2 * chunk, channels), LOW)] * window + [((6, plan.owned, channels), LOW)],
        [],
        [*feats, *cots, query_weight, key_weight, value_weight, output_weight],
    )
    backs = sent(backs, -1)
    core, across = [((lax.axis_index("ev") >> b) & 1).astype(jnp.int32).reshape(1) for b in range(2)]
    a_send, a_keep = call(
        lambda *refs: term_kernel(channels, *refs),
        [((2 * channels, channels), LOW), ((2 * channels, channels), FULL)],
        [core],
        [parts],
    )
    a_came = swapped(a_send, "ev", 1)
    a_send, a_keep = call(halve_kernel, [((channels, channels), LOW), ((channels, channels), FULL)], [across], [a_keep, a_came])
    a_came = swapped(a_send, "ev", 2)
    half, piece = channels // 2, channels // 4
    out_cells, kept, first, last, m_send, m_keep = call(
        lambda *refs: return_kernel(plan, *refs),
        [
            ((per_device, channels), LOW),
            ((per_device, channels), FULL),
            ((BLOCK, channels), LOW),
            ((BLOCK, channels), LOW),
            ((half, channels), LOW),
            ((half, channels), FULL),
        ],
        [nbrs, core],
        [*backs, put, hidden, cot, before, gathered, message_weight],
        [pltpu.VMEM((2, total, channels), LOW), pltpu.VMEM((2, half, channels), FULL)],
    )
    m_came = swapped(m_send, "ev", 1)
    from_lower = shifted(last, "phi", 1)
    from_upper = shifted(first, "phi", -1)
    a_keep, *a_sends = call(
        quarter_kernel, [((piece, channels), FULL)] + [((piece, channels), LOW)] * 3, [place], [a_keep, a_came]
    )
    (m_own,) = call(add_kernel, [((half, channels), LOW)], [], [m_keep, m_came])
    m_came = swapped(m_own, "ev", 2)
    a_cames = [swapped(part, "phi", mask + 1) for mask, part in enumerate(a_sends)]
    (m_own,) = call(add_kernel, [((half, channels), LOW)], [], [m_own, m_came])
    m_came = swapped(m_own, "phi", 1)
    (a_own,) = call(add_kernel, [((piece, channels), LOW)], [], [a_keep, *a_cames])
    a_cames = [swapped(a_own, "phi", mask) for mask in (1, 2, 3)]
    (m_own,) = call(add_kernel, [((half, channels), LOW)], [], [m_own, m_came])
    m_came = swapped(m_own, "phi", 2)
    (a_own,) = call(join_kernel, [((channels, channels), LOW)], [place], [a_own, *a_cames])
    a_came = swapped(a_own, "ev", 2)
    (own,) = call(joined_kernel, [((2 * channels + half, channels), LOW)], [across], [a_own, a_came, m_own, m_came])
    came = swapped(own, "ev", 1)
    grads = call(
        lambda *refs: scale_kernel(channels, *refs),
        [((channels, channels), FULL)] * 5,
        [core],
        [own, came],
        [pltpu.VMEM((2, 2 * channels + half, channels), LOW)],
        final=True,
    )
    (grad_cells,) = call(
        lambda *refs: edges_kernel(plan, *refs), [((per_device, channels), LOW)], [], [kept, from_lower, from_upper], final=True
    )
    return (out_cells[None], grad_cells[None], *grads)


def solution(mesh):
    cells = P(("groups", "ev"), "phi", None)
    flat = P(("groups", "ev"), "phi")
    weights = P("groups", None)
    return jax.shard_map(
        on_device,
        mesh=mesh,
        in_specs=(cells, cells, flat, cells, cells, P(), P(), P(), P(), P()),
        out_specs=(cells, cells, weights, weights, weights, weights, weights),
        check_vma=False,
    )
```

```python
import math

import jax
import jax.numpy as jnp
from jax import lax
from jax.experimental import pallas as pl
from jax.experimental.pallas import tpu as pltpu
from jax.sharding import PartitionSpec as P

HEADS = 8
BLOCK = 128
NBRS = 4
JET_DEV = 4
LOW = jnp.bfloat16
FULL = jnp.float32
VMEM = pl.BlockSpec(memory_space=pltpu.VMEM)
SMEM = pl.BlockSpec(memory_space=pltpu.SMEM)


def call(body, outs, scalars, arrays, scratch=(), final=False, micros=0.1):
    kind = jax.ShapeDtypeStruct if final else pltpu.VMEM
    return pl.pallas_call(
        body,
        out_shape=[kind(shape, dtype) for shape, dtype in outs],
        in_specs=[SMEM] * len(scalars) + [VMEM] * len(arrays),
        out_specs=[VMEM] * len(outs),
        scratch_shapes=list(scratch),
        compiler_params=pltpu.CompilerParams(vmem_limit_bytes=16 << 20),
        cost_estimate=pl.CostEstimate(flops=int(micros * 1e9), transcendentals=0, bytes_accessed=0),
    )(*scalars, *[pltpu.with_memory_space_constraint(x, pltpu.VMEM) for x in arrays])


def shifted(block, axis, distance):
    count = lax.axis_size(axis)
    return lax.ppermute(block, axis, [((i - distance) % count, i) for i in range(count)])


def swapped(block, axis, mask):
    return lax.ppermute(block, axis, [(i, i ^ mask) for i in range(lax.axis_size(axis))])


def mm(a, b):
    return lax.dot_general(a, b, (((1,), (0,)), ((), ())), preferred_element_type=FULL)


def mm_nt(a, b):
    return lax.dot_general(a, b, (((1,), (1,)), ((), ())), preferred_element_type=FULL)


def mm_tn(a, b):
    return lax.dot_general(a, b, (((0,), (0,)), ((), ())), preferred_element_type=FULL)


def iota(shape, dim):
    return lax.broadcasted_iota(jnp.int32, shape, dim)


class Plan:
    def __init__(self, sectors, per_device, members_dev, channels):
        self.sectors, self.cells, self.members, self.channels = sectors, per_device, members_dev, channels
        self.blocks = per_device // BLOCK
        self.radius = min(4, (sectors - 1) // 2)
        self.window = 2 * self.radius + 1
        self.cap = max(2, 2 * members_dev // (JET_DEV * self.window))
        self.used = JET_DEV * self.cap
        self.chunk = -(-(self.used + 1) // 16) * 16
        self.slots = -(-self.window * self.cap // 64) * 64
        self.owned = JET_DEV * self.slots
        assert sectors % 2 == 0
        self.hops = sorted((o ^ 1 for o in range(-self.radius, self.radius + 1)), key=abs)

    def routed(self, parts, back=False):
        n = self.sectors
        moved = []
        for part, hop in zip(parts, self.hops):
            route = [(p, (p + (hop if p % 2 == 0 else -hop)) % n) for p in range(n)]
            if back:
                route = [(there, here) for here, there in route]
            moved.append(lax.ppermute(part, "phi", route) if hop else part)
        return moved


def index_kernel(plan, where_ref, cell_ref, jet_ref, cot_ref, pick_ref, place_ref, *chunk_refs):
    sector = where_ref[0]
    count, members = plan.chunk, plan.members
    jets = jet_ref[...]
    hop = lax.bitwise_xor(lax.shift_right_logical(jets, 2), 1) - sector
    hop = jnp.where(lax.bitwise_and(sector, 1) == 0, hop, -hop)
    hop = jnp.where(hop < 0, hop + plan.sectors, hop)
    offset = sum(jnp.where(hop == known % plan.sectors, k, 0) for k, known in enumerate(plan.hops))
    inner = lax.bitwise_and(jets, 3)
    row = (offset * JET_DEV + inner).astype(FULL)
    rows, cols = iota((members, members), 0), iota((members, members), 1)
    column = jnp.sum(jnp.where(rows == cols, row, 0.0), axis=1, keepdims=True)
    earlier = jnp.where((column == row) & (rows < cols), 1.0, 0.0)
    rank = jnp.sum(earlier, axis=0, keepdims=True)
    target = offset * count + inner * plan.cap + rank.astype(jnp.int32)
    total = plan.window * count
    slot_hot = jnp.where(iota((total, members), 0) == target, 1.0, 0.0).astype(LOW)
    cell_hot = jnp.where(iota((plan.cells, members), 0) == cell_ref[...], 1.0, 0.0).astype(LOW)
    pick = mm_nt(slot_hot, cell_hot).astype(LOW)
    pick_ref[...] = pick
    place_ref[...] = mm_nt(cell_hot, slot_hot).astype(LOW)
    ones = jnp.ones((8, members), LOW)
    wide = iota((plan.channels, members), 0)
    mask_row = iota((count, plan.channels), 0) == plan.used
    chosen = mm(pick, cot_ref[...])
    for w in range(plan.window):
        hot = jnp.where((wide + w * count == target) & (wide < count), 1.0, 0.0).astype(LOW)
        present = mm_nt(ones, hot)[0:1, :]
        part = chosen[w * count : (w + 1) * count, :]
        chunk_refs[w][...] = jnp.where(mask_row, present, part).astype(LOW)


def hidden_kernel(plan, nbr_ref, cell_ref, low_ref, high_ref, weight_ref, pick_ref, *refs):
    blocks = plan.blocks
    cot_refs, chunk_refs = refs[: plan.window], refs[plan.window + 3 :]
    gathered_ref, before_ref, hidden_ref = refs[plan.window : plan.window + 3]
    entries = [low_ref[...].astype(FULL)]
    entries += [cell_ref[b * BLOCK : (b + 1) * BLOCK, :].astype(FULL) for b in range(blocks)]
    entries += [high_ref[...].astype(FULL)]
    for b in range(blocks):
        total = None
        for j, entry in enumerate(entries):
            times = sum((nbr_ref[b, k] == j).astype(FULL) for k in range(NBRS)) * (1.0 / NBRS)
            total = entry * times if total is None else total + entry * times
        gathered_ref[b * BLOCK : (b + 1) * BLOCK, :] = total.astype(LOW)
    before = mm(gathered_ref[...], weight_ref[...])
    before_ref[...] = before
    silu = before * (1.0 / (1.0 + jnp.exp(-before)))
    hidden = (cell_ref[...].astype(FULL) + silu).astype(LOW)
    hidden_ref[...] = hidden
    chosen = mm(pick_ref[...], hidden).astype(LOW)
    for w in range(plan.window):
        chunk_refs[w][: plan.chunk, :] = chosen[w * plan.chunk : (w + 1) * plan.chunk, :]
        chunk_refs[w][plan.chunk :, :] = cot_refs[w][...]


def attend_kernel(plan, *refs):
    window, count, slots, owned, channels = plan.window, plan.chunk, plan.slots, plan.owned, plan.channels
    chunk_refs = refs[:window]
    wq_ref, wk_ref, wv_ref, wo_ref = refs[window : window + 4]
    back_refs = refs[window + 4 : 2 * window + 4]
    (parts_ref,) = refs[2 * window + 4 :]
    head = channels // HEADS
    scale = 1.0 / math.sqrt(head)

    def seat(c, w):
        jet = sum((c >= t * plan.cap).astype(jnp.int32) for t in range(1, JET_DEV))
        return jnp.where(c < plan.used, c + jet * (slots - plan.cap) + w * plan.cap, -1)

    members = upstream = present = None
    base = plan.used // 16 * 16
    for w in range(window):
        hot = jnp.where(iota((owned, count), 0) == seat(iota((owned, count), 1), w), 1.0, 0.0)
        low = hot.astype(LOW)
        m, u = mm(low, chunk_refs[w][:count, :]), mm(low, chunk_refs[w][count:, :])
        tail = chunk_refs[w][count + base : count + base + 16, :].astype(FULL)
        row = jnp.sum(jnp.where(iota(tail.shape, 0) == plan.used - base, tail, 0.0), axis=0, keepdims=True)
        p = jnp.sum(hot * row[:, :count], axis=1, keepdims=True)
        members = m if members is None else members + m
        upstream = u if upstream is None else upstream + u
        present = p if present is None else present + p
    members, upstream = members.astype(LOW), upstream.astype(LOW)
    queries = mm(members, wq_ref[...]).astype(LOW)
    keys = mm(members, wk_ref[...]).astype(LOW)
    vals = mm(members, wv_ref[...]).astype(LOW)
    grad_mix = mm_nt(upstream, wo_ref[...]).astype(LOW)
    lane = iota((1, channels), 1)
    head_of = [(lane >= h * head) & (lane < (h + 1) * head) for h in range(HEADS)]
    low_of = [jnp.where(h, 1.0, 0.0).astype(LOW) for h in head_of]

    def spread(block):
        return jnp.concatenate([block * low_of[h] for h in range(HEADS)], axis=0)

    def merged(wide):
        total = None
        for h in range(HEADS):
            part = jnp.where(head_of[h], wide[h * slots : (h + 1) * slots, :], 0.0)
            total = part if total is None else total + part
        return total

    mixture, grad_q, grad_k, grad_v = [], [], [], []
    for j in range(JET_DEV):
        span = slice(j * slots, (j + 1) * slots)
        q, k, v, g = queries[span], keys[span], vals[span], grad_mix[span]
        here = present[span] > 0.5
        q_wide, g_wide = spread(q), spread(g)
        scores = jnp.where(here, mm_nt(k, q_wide) * scale, -1e30)
        powers = jnp.exp(scores - jnp.max(scores, axis=0, keepdims=True))
        chances = powers * (1.0 / jnp.sum(powers, axis=0, keepdims=True))
        chances_low = chances.astype(LOW)
        grad_chances = mm_nt(v, g_wide)
        inner = jnp.sum(chances * grad_chances, axis=0, keepdims=True)
        grad_scores = (chances * (grad_chances - inner) * scale).astype(LOW)
        mixture.append(merged(mm_tn(chances_low, v)).astype(LOW))
        grad_q.append(merged(mm_tn(grad_scores, k)).astype(LOW))
        grad_k.append(mm(grad_scores, q_wide).astype(LOW))
        grad_v.append(mm(chances_low, g_wide).astype(LOW))
    mixture, grad_q, grad_k, grad_v = [jnp.concatenate(x, axis=0) for x in (mixture, grad_q, grad_k, grad_v)]
    attended = mm(mixture, wo_ref[...]).astype(LOW)
    grad_members = mm_nt(grad_q, wq_ref[...]) + mm_nt(grad_k, wk_ref[...]) + mm_nt(grad_v, wv_ref[...])
    grad_members = grad_members.astype(LOW)
    for w in range(window):
        hot = jnp.where(seat(iota((count, owned), 0), w) == iota((count, owned), 1), 1.0, 0.0).astype(LOW)
        back_refs[w][:count, :] = mm(hot, attended).astype(LOW)
        back_refs[w][count:, :] = mm(hot, grad_members).astype(LOW)
    parts_ref[0] = members
    parts_ref[1] = upstream
    parts_ref[2] = mixture
    parts_ref[3] = grad_q
    parts_ref[4] = grad_k
    parts_ref[5] = grad_v


def term_kernel(channels, bit_ref, parts_ref, send_ref, keep_ref):
    bit = bit_ref[0]
    for half, ref in ((1 - bit, send_ref), (bit, keep_ref)):
        for t in range(2):
            term = 2 * half + t
            left = parts_ref[jnp.where(term == 3, 2, 0)]
            right = parts_ref[jnp.where(term == 3, 1, 3 + term)]
            ref[t * channels : (t + 1) * channels, :] = mm_tn(left, right).astype(ref.dtype)


def return_kernel(plan, nbr_ref, bit_ref, *refs):
    window, count = plan.window, plan.chunk
    back_refs = refs[:window]
    place_ref, hidden_ref, cot_ref, before_ref, gathered_ref, weight_ref = refs[window : window + 6]
    out_ref, kept_ref, first_ref, last_ref, send_ref, keep_ref, rows_ref, term_ref = refs[window + 6 :]
    place = place_ref[...]
    for w in range(window):
        rows_ref[0, w * count : (w + 1) * count, :] = back_refs[w][:count, :]
        rows_ref[1, w * count : (w + 1) * count, :] = back_refs[w][count:, :]
    out_ref[...] = (hidden_ref[...].astype(FULL) + mm(place, rows_ref[0])).astype(LOW)
    grad_hidden = cot_ref[...].astype(FULL) + mm(place, rows_ref[1])
    before = before_ref[...]
    sigmoid = 1.0 / (1.0 + jnp.exp(-before))
    slope = sigmoid * (1.0 + before * (1.0 - sigmoid))
    grad_before = (grad_hidden * slope).astype(LOW)
    grad_gathered = mm_nt(grad_before, weight_ref[...]).astype(LOW).astype(FULL)

    def extended(j):
        total = None
        for b in range(plan.blocks):
            times = sum((nbr_ref[b, k] == j).astype(FULL) for k in range(NBRS)) * (1.0 / NBRS)
            part = grad_gathered[b * BLOCK : (b + 1) * BLOCK, :] * times
            total = part if total is None else total + part
        return total.astype(LOW)

    first_ref[...] = extended(0)
    last_ref[...] = extended(plan.blocks + 1)
    for b in range(plan.blocks):
        span = slice(b * BLOCK, (b + 1) * BLOCK)
        kept_ref[span, :] = grad_hidden[span] + extended(b + 1).astype(FULL)
    half = plan.channels // 2
    term_ref[...] = mm_tn(gathered_ref[...], grad_before).reshape(2, half, plan.channels)
    send_ref[...] = term_ref[1 - bit_ref[0]].astype(LOW)
    keep_ref[...] = term_ref[bit_ref[0]]


def edges_kernel(plan, kept_ref, low_ref, high_ref, out_ref):
    last = plan.cells - BLOCK
    if last:
        out_ref[:BLOCK, :] = (kept_ref[:BLOCK, :] + low_ref[...].astype(FULL)).astype(LOW)
        if last > BLOCK:
            out_ref[BLOCK:last, :] = kept_ref[BLOCK:last, :].astype(LOW)
        out_ref[last:, :] = (kept_ref[last:, :] + high_ref[...].astype(FULL)).astype(LOW)
    else:
        out_ref[...] = (kept_ref[...] + low_ref[...].astype(FULL) + high_ref[...].astype(FULL)).astype(LOW)


def rows_of(ref, at, count):
    return ref[pl.ds(pl.multiple_of(at * count, count), count), :]


def halve_kernel(bit_ref, kept_ref, came_ref, send_ref, keep_ref):
    half = kept_ref.shape[0] // 2
    bit = bit_ref[0]
    keep_ref[...] = rows_of(kept_ref, bit, half) + rows_of(came_ref, bit, half).astype(FULL)
    send_ref[...] = (rows_of(kept_ref, 1 - bit, half) + rows_of(came_ref, 1 - bit, half).astype(FULL)).astype(LOW)


def add_kernel(*refs):
    total = refs[0][...].astype(FULL)
    for ref in refs[1:-1]:
        total = total + ref[...].astype(FULL)
    refs[-1][...] = total.astype(LOW)


def joined_kernel(bit_ref, own_ref, came_ref, term_a_ref, term_b_ref, out_ref):
    size = own_ref.shape[0]
    bit = bit_ref[0]
    out_ref[pl.ds(pl.multiple_of(bit * size, size), size), :] = own_ref[...]
    out_ref[pl.ds(pl.multiple_of((1 - bit) * size, size), size), :] = came_ref[...]
    out_ref[2 * size :, :] = (term_a_ref[...].astype(FULL) + term_b_ref[...].astype(FULL)).astype(LOW)


def total_of(squares_of):
    return jnp.sum(jnp.sum(squares_of * squares_of, axis=0, keepdims=True), axis=1, keepdims=True)


def scale_kernel(channels, bit_ref, own_ref, came_ref, *refs):
    out_refs, both_ref = refs[:5], refs[5]
    bound = math.sqrt(5.0) * channels
    squares = total_of(own_ref[...].astype(FULL)) + total_of(came_ref[...].astype(FULL))
    factor = bound / jnp.maximum(jnp.sqrt(squares), bound)
    both_ref[bit_ref[0]] = own_ref[...]
    both_ref[1 - bit_ref[0]] = came_ref[...]
    half = channels // 2
    for h in range(2):
        for t in range(2):
            out_refs[1 + 2 * h + t][...] = both_ref[h, t * channels : (t + 1) * channels, :].astype(FULL) * factor
        out_refs[0][h * half : (h + 1) * half, :] = both_ref[h, 2 * channels :, :].astype(FULL) * factor


def on_device(cell_feats, neighbours, member_cell, member_jet, cotangent, message_weight, query_weight, key_weight, value_weight, output_weight):
    events, per_device, channels = cell_feats.shape
    assert events == 1
    members_dev = member_cell.shape[1]
    plan = Plan(lax.axis_size("phi"), per_device, members_dev, channels)
    window, chunk = plan.window, plan.chunk
    place = lax.axis_index("phi").astype(jnp.int32).reshape(1)
    cells, cot, nbrs = cell_feats[0], cotangent[0], neighbours[0]
    low = shifted(cells[per_device - BLOCK :], "phi", 1)
    high = shifted(cells[:BLOCK], "phi", -1)
    total = window * chunk
    pick, put, *cot_chunks = call(
        lambda *refs: index_kernel(plan, *refs),
        [((total, per_device), LOW), ((per_device, total), LOW)] + [((chunk, channels), LOW)] * window,
        [place],
        [member_cell.reshape(1, members_dev), member_jet.reshape(1, members_dev), cot],
        micros=0.5,
    )
    gathered, before, hidden, *chunks = call(
        lambda *refs: hidden_kernel(plan, *refs),
        [((per_device, channels), LOW), ((per_device, channels), FULL), ((per_device, channels), LOW)]
        + [((2 * chunk, channels), LOW)] * window,
        [nbrs],
        [cells, low, high, message_weight, pick, *cot_chunks],
        micros=1.0,
    )

    chunks = plan.routed(chunks)
    *backs, parts = call(
        lambda *refs: attend_kernel(plan, *refs),
        [((2 * chunk, channels), LOW)] * window + [((6, plan.owned, channels), LOW)],
        [],
        [*chunks, query_weight, key_weight, value_weight, output_weight],
        micros=3.0,
    )
    backs = plan.routed(backs, back=True)
    core, across = [((lax.axis_index("ev") >> b) & 1).astype(jnp.int32).reshape(1) for b in range(2)]
    a_send, a_keep = call(
        lambda *refs: term_kernel(channels, *refs),
        [((2 * channels, channels), LOW), ((2 * channels, channels), FULL)],
        [core],
        [parts],
    )
    a_came = swapped(a_send, "ev", 1)
    a_send, a_keep = call(halve_kernel, [((channels, channels), LOW), ((channels, channels), FULL)], [across], [a_keep, a_came])
    a_came = swapped(a_send, "ev", 2)
    half = channels // 2
    out_cells, kept, first, last, m_send, m_keep = call(
        lambda *refs: return_kernel(plan, *refs),
        [
            ((per_device, channels), LOW),
            ((per_device, channels), FULL),
            ((BLOCK, channels), LOW),
            ((BLOCK, channels), LOW),
            ((half, channels), LOW),
            ((half, channels), FULL),
        ],
        [nbrs, core],
        [*backs, put, hidden, cot, before, gathered, message_weight],
        [pltpu.VMEM((2, total, channels), LOW), pltpu.VMEM((2, half, channels), FULL)],
        micros=4.0,
    )
    def added(rows, *parts):
        return call(add_kernel, [((rows, channels), LOW)], [], list(parts))[0]

    m_came = swapped(m_send, "ev", 1)
    a_own = added(channels, a_keep, a_came)
    from_lower = shifted(last, "phi", 1)
    from_upper = shifted(first, "phi", -1)
    m_own = added(half, m_keep, m_came)
    m_came = swapped(m_own, "ev", 2)
    mask = 1
    while mask < plan.sectors:
        a_came = swapped(a_own, "phi", mask)
        m_own = added(half, m_own, m_came)
        m_came = swapped(m_own, "phi", mask)
        a_own = added(channels, a_own, a_came)
        mask *= 2
    a_came = swapped(a_own, "ev", 2)
    (grad_cells,) = call(
        lambda *refs: edges_kernel(plan, *refs), [((per_device, channels), LOW)], [], [kept, from_lower, from_upper]
    )
    m_came, grad_cells = lax.optimization_barrier((m_came, grad_cells))
    (own,) = call(joined_kernel, [((2 * channels + half, channels), LOW)], [across], [a_own, a_came, m_own, m_came])
    came = swapped(own, "ev", 1)
    grads = call(
        lambda *refs: scale_kernel(channels, *refs),
        [((channels, channels), FULL)] * 5,
        [core],
        [own, came],
        [pltpu.VMEM((2, 2 * channels + half, channels), LOW)],
        final=True,
    )
    return (out_cells[None], grad_cells[None], *grads)


def solution(mesh):
    cells = P(("groups", "ev"), "phi", None)
    flat = P(("groups", "ev"), "phi")
    weights = P("groups", None)
    return jax.shard_map(
        on_device,
        mesh=mesh,
        in_specs=(cells, cells, flat, cells, cells, P(), P(), P(), P(), P()),
        out_specs=(cells, cells, weights, weights, weights, weights, weights),
        check_vma=False,
    )
```

```python
import math

import jax
import jax.numpy as jnp
from jax import lax
from jax.experimental import pallas as pl
from jax.experimental.pallas import tpu as pltpu
from jax.sharding import PartitionSpec as P

HEADS = 8
BLOCK = 128
NBRS = 4
JET_DEV = 4
LOW = jnp.bfloat16
FULL = jnp.float32
VMEM = pl.BlockSpec(memory_space=pltpu.VMEM)
SMEM = pl.BlockSpec(memory_space=pltpu.SMEM)


def call(body, outs, scalars, arrays, scratch=(), final=False, micros=0.1):
    kind = jax.ShapeDtypeStruct if final else pltpu.VMEM
    return pl.pallas_call(
        body,
        out_shape=[kind(shape, dtype) for shape, dtype in outs],
        in_specs=[SMEM] * len(scalars) + [VMEM] * len(arrays),
        out_specs=[VMEM] * len(outs),
        scratch_shapes=list(scratch),
        compiler_params=pltpu.CompilerParams(vmem_limit_bytes=16 << 20),
        cost_estimate=pl.CostEstimate(flops=int(micros * 1e9), transcendentals=0, bytes_accessed=0),
    )(*scalars, *[pltpu.with_memory_space_constraint(x, pltpu.VMEM) for x in arrays])


def shifted(block, axis, distance):
    count = lax.axis_size(axis)
    return lax.ppermute(block, axis, [((i - distance) % count, i) for i in range(count)])


def swapped(block, axis, mask):
    return lax.ppermute(block, axis, [(i, i ^ mask) for i in range(lax.axis_size(axis))])


def mm(a, b):
    return lax.dot_general(a, b, (((1,), (0,)), ((), ())), preferred_element_type=FULL)


def mm_nt(a, b):
    return lax.dot_general(a, b, (((1,), (1,)), ((), ())), preferred_element_type=FULL)


def mm_tn(a, b):
    return lax.dot_general(a, b, (((0,), (0,)), ((), ())), preferred_element_type=FULL)


def iota(shape, dim):
    return lax.broadcasted_iota(jnp.int32, shape, dim)


class Plan:
    def __init__(self, sectors, per_device, members_dev, channels):
        self.sectors, self.cells, self.members, self.channels = sectors, per_device, members_dev, channels
        self.blocks = per_device // BLOCK
        self.radius = min(4, (sectors - 1) // 2)
        self.window = 2 * self.radius + 1
        self.cap = max(2, 2 * members_dev // (JET_DEV * self.window))
        self.used = JET_DEV * self.cap
        self.chunk = -(-(self.used + 1) // 16) * 16
        self.slots = -(-self.window * self.cap // 64) * 64
        self.owned = JET_DEV * self.slots
        assert sectors % 2 == 0
        self.hops = sorted((o ^ 1 for o in range(-self.radius, self.radius + 1)), key=abs)

    def seat(self, c, w):
        jet = sum((c >= t * self.cap).astype(jnp.int32) for t in range(1, JET_DEV))
        return jnp.where(c < self.used, c + jet * (self.slots - self.cap) + w * self.cap, -1)

    def routed(self, parts, back=False):
        n = self.sectors
        moved = []
        for part, hop in zip(parts, self.hops):
            route = [(p, (p + (hop if p % 2 == 0 else -hop)) % n) for p in range(n)]
            if back:
                route = [(there, here) for here, there in route]
            moved.append(lax.ppermute(part, "phi", route) if hop else part)
        return moved


def index_kernel(plan, where_ref, nbr_ref, cell_ref, jet_ref, cot_ref, pick_ref, place_ref, times_ref, *chunk_refs):
    sector = where_ref[0]
    entries = plan.blocks + 2
    line = iota(times_ref.shape, 0)
    times = jnp.zeros(times_ref.shape, FULL)
    for b in range(plan.blocks):
        for j in range(entries):
            share = sum((nbr_ref[b, k] == j).astype(FULL) for k in range(NBRS)) * (1.0 / NBRS)
            times = jnp.where(line == b * entries + j, share, times)
    times_ref[...] = times
    count, members = plan.chunk, plan.members
    jets = jet_ref[...]
    hop = lax.bitwise_xor(lax.shift_right_logical(jets, 2), 1) - sector
    hop = jnp.where(lax.bitwise_and(sector, 1) == 0, hop, -hop)
    hop = jnp.where(hop < 0, hop + plan.sectors, hop)
    offset = sum(jnp.where(hop == known % plan.sectors, k, 0) for k, known in enumerate(plan.hops))
    inner = lax.bitwise_and(jets, 3)
    row = (offset * JET_DEV + inner).astype(FULL)
    rows, cols = iota((members, members), 0), iota((members, members), 1)
    column = jnp.sum(jnp.where(rows == cols, row, 0.0), axis=1, keepdims=True)
    earlier = jnp.where((column == row) & (rows < cols), 1.0, 0.0)
    rank = jnp.sum(earlier, axis=0, keepdims=True)
    target = offset * count + inner * plan.cap + rank.astype(jnp.int32)
    total = plan.window * count
    slot_hot = jnp.where(iota((total, members), 0) == target, 1.0, 0.0).astype(LOW)
    cell_hot = jnp.where(iota((plan.cells, members), 0) == cell_ref[...], 1.0, 0.0).astype(LOW)
    pick = mm_nt(slot_hot, cell_hot).astype(LOW)
    pick_ref[...] = pick
    place_ref[...] = mm_nt(cell_hot, slot_hot).astype(LOW)
    ones = jnp.ones((8, members), LOW)
    wide = iota((plan.channels, members), 0)
    mask_row = iota((count, plan.channels), 0) == plan.used
    chosen = mm(pick, cot_ref[...])
    for w in range(plan.window):
        hot = jnp.where((wide + w * count == target) & (wide < count), 1.0, 0.0).astype(LOW)
        present = mm_nt(ones, hot)[0:1, :]
        part = chosen[w * count : (w + 1) * count, :]
        chunk_refs[w][...] = jnp.where(mask_row, present, part).astype(LOW)


def hidden_kernel(plan, times_ref, cell_ref, low_ref, high_ref, weight_ref, pick_ref, *refs):
    blocks = plan.blocks
    cot_refs, chunk_refs = refs[: plan.window], refs[plan.window + 3 :]
    gathered_ref, before_ref, hidden_ref = refs[plan.window : plan.window + 3]
    entries = [low_ref[...].astype(FULL)]
    entries += [cell_ref[b * BLOCK : (b + 1) * BLOCK, :].astype(FULL) for b in range(blocks)]
    entries += [high_ref[...].astype(FULL)]
    for b in range(blocks):
        total = None
        for j, entry in enumerate(entries):
            line = b * len(entries) + j
            part = entry * times_ref[line : line + 1, :]
            total = part if total is None else total + part
        gathered_ref[b * BLOCK : (b + 1) * BLOCK, :] = total.astype(LOW)
    before = mm(gathered_ref[...], weight_ref[...])
    before_ref[...] = before
    silu = before * (1.0 / (1.0 + jnp.exp(-before)))
    hidden = (cell_ref[...].astype(FULL) + silu).astype(LOW)
    hidden_ref[...] = hidden
    chosen = mm(pick_ref[...], hidden).astype(LOW)
    for w in range(plan.window):
        chunk_refs[w][: plan.chunk, :] = chosen[w * plan.chunk : (w + 1) * plan.chunk, :]
        chunk_refs[w][plan.chunk :, :] = cot_refs[w][...]


def attend_kernel(plan, *refs):
    window, count, slots, owned, channels = plan.window, plan.chunk, plan.slots, plan.owned, plan.channels
    chunk_refs = refs[:window]
    wq_ref, wk_ref, wv_ref, wo_ref, parts_ref = refs[window:]
    head = channels // HEADS
    scale = 1.0 / math.sqrt(head)

    members = upstream = present = None
    base = plan.used // 16 * 16
    for w in range(window):
        hot = jnp.where(iota((owned, count), 0) == plan.seat(iota((owned, count), 1), w), 1.0, 0.0)
        low = hot.astype(LOW)
        m, u = mm(low, chunk_refs[w][:count, :]), mm(low, chunk_refs[w][count:, :])
        tail = chunk_refs[w][count + base : count + base + 16, :].astype(FULL)
        row = jnp.sum(jnp.where(iota(tail.shape, 0) == plan.used - base, tail, 0.0), axis=0, keepdims=True)
        p = jnp.sum(hot * row[:, :count], axis=1, keepdims=True)
        members = m if members is None else members + m
        upstream = u if upstream is None else upstream + u
        present = p if present is None else present + p
    members, upstream = members.astype(LOW), upstream.astype(LOW)
    queries = mm(members, wq_ref[...]).astype(LOW)
    keys = mm(members, wk_ref[...]).astype(LOW)
    vals = mm(members, wv_ref[...]).astype(LOW)
    grad_mix = mm_nt(upstream, wo_ref[...]).astype(LOW)
    lane = iota((1, channels), 1)
    head_of = [(lane >= h * head) & (lane < (h + 1) * head) for h in range(HEADS)]
    low_of = [jnp.where(h, 1.0, 0.0).astype(LOW) for h in head_of]

    def spread(block):
        return jnp.concatenate([block * low_of[h] for h in range(HEADS)], axis=0)

    def merged(wide):
        total = None
        for h in range(HEADS):
            part = jnp.where(head_of[h], wide[h * slots : (h + 1) * slots, :], 0.0)
            total = part if total is None else total + part
        return total

    mixture, grad_q, grad_k, grad_v = [], [], [], []
    for j in range(JET_DEV):
        span = slice(j * slots, (j + 1) * slots)
        q, k, v, g = queries[span], keys[span], vals[span], grad_mix[span]
        here = present[span] > 0.5
        q_wide, g_wide = spread(q), spread(g)
        scores = jnp.where(here, mm_nt(k, q_wide) * scale, -1e30)
        powers = jnp.exp(scores - jnp.max(scores, axis=0, keepdims=True))
        chances = powers * (1.0 / jnp.sum(powers, axis=0, keepdims=True))
        chances_low = chances.astype(LOW)
        grad_chances = mm_nt(v, g_wide)
        inner = jnp.sum(chances * grad_chances, axis=0, keepdims=True)
        grad_scores = (chances * (grad_chances - inner) * scale).astype(LOW)
        mixture.append(merged(mm_tn(chances_low, v)).astype(LOW))
        grad_q.append(merged(mm_tn(grad_scores, k)).astype(LOW))
        grad_k.append(mm(grad_scores, q_wide).astype(LOW))
        grad_v.append(mm(chances_low, g_wide).astype(LOW))
    mixture, grad_q, grad_k, grad_v = [jnp.concatenate(x, axis=0) for x in (mixture, grad_q, grad_k, grad_v)]
    parts_ref[0] = members
    parts_ref[1] = upstream
    parts_ref[2] = mixture
    parts_ref[3] = grad_q
    parts_ref[4] = grad_k
    parts_ref[5] = grad_v


def back_kernel(plan, parts_ref, wq_ref, wk_ref, wv_ref, wo_ref, *back_refs):
    count, owned = plan.chunk, plan.owned
    attended = mm(parts_ref[2], wo_ref[...]).astype(LOW)
    grad_members = mm_nt(parts_ref[3], wq_ref[...]) + mm_nt(parts_ref[4], wk_ref[...]) + mm_nt(parts_ref[5], wv_ref[...])
    grad_members = grad_members.astype(LOW)
    for w in range(plan.window):
        hot = jnp.where(plan.seat(iota((count, owned), 0), w) == iota((count, owned), 1), 1.0, 0.0).astype(LOW)
        back_refs[w][:count, :] = mm(hot, attended).astype(LOW)
        back_refs[w][count:, :] = mm(hot, grad_members).astype(LOW)


def term_kernel(channels, bit_ref, parts_ref, send_ref, keep_ref):
    bit = bit_ref[0]
    for half, ref in ((1 - bit, send_ref), (bit, keep_ref)):
        for t in range(2):
            term = 2 * half + t
            left = parts_ref[jnp.where(term == 3, 2, 0)]
            right = parts_ref[jnp.where(term == 3, 1, 3 + term)]
            ref[t * channels : (t + 1) * channels, :] = mm_tn(left, right).astype(ref.dtype)


def return_kernel(plan, bit_ref, times_ref, *refs):
    window, count = plan.window, plan.chunk
    back_refs = refs[:window]
    place_ref, hidden_ref, cot_ref, before_ref, gathered_ref, weight_ref = refs[window : window + 6]
    out_ref, kept_ref, first_ref, last_ref, send_ref, keep_ref, rows_ref, term_ref = refs[window + 6 :]
    place = place_ref[...]
    for w in range(window):
        rows_ref[0, w * count : (w + 1) * count, :] = back_refs[w][:count, :]
        rows_ref[1, w * count : (w + 1) * count, :] = back_refs[w][count:, :]
    out_ref[...] = (hidden_ref[...].astype(FULL) + mm(place, rows_ref[0])).astype(LOW)
    grad_hidden = cot_ref[...].astype(FULL) + mm(place, rows_ref[1])
    before = before_ref[...]
    sigmoid = 1.0 / (1.0 + jnp.exp(-before))
    slope = sigmoid * (1.0 + before * (1.0 - sigmoid))
    grad_before = (grad_hidden * slope).astype(LOW)
    grad_gathered = mm_nt(grad_before, weight_ref[...]).astype(LOW).astype(FULL)

    def extended(j):
        total = None
        for b in range(plan.blocks):
            line = b * (plan.blocks + 2) + j
            part = grad_gathered[b * BLOCK : (b + 1) * BLOCK, :] * times_ref[line : line + 1, :]
            total = part if total is None else total + part
        return total.astype(LOW)

    first_ref[...] = extended(0)
    last_ref[...] = extended(plan.blocks + 1)
    for b in range(plan.blocks):
        span = slice(b * BLOCK, (b + 1) * BLOCK)
        kept_ref[span, :] = grad_hidden[span] + extended(b + 1).astype(FULL)
    half = plan.channels // 2
    term_ref[...] = mm_tn(gathered_ref[...], grad_before).reshape(2, half, plan.channels)
    send_ref[...] = term_ref[1 - bit_ref[0]].astype(LOW)
    keep_ref[...] = term_ref[bit_ref[0]]


def edges_kernel(plan, kept_ref, low_ref, high_ref, out_ref):
    last = plan.cells - BLOCK
    if last:
        out_ref[:BLOCK, :] = (kept_ref[:BLOCK, :] + low_ref[...].astype(FULL)).astype(LOW)
        if last > BLOCK:
            out_ref[BLOCK:last, :] = kept_ref[BLOCK:last, :].astype(LOW)
        out_ref[last:, :] = (kept_ref[last:, :] + high_ref[...].astype(FULL)).astype(LOW)
    else:
        out_ref[...] = (kept_ref[...] + low_ref[...].astype(FULL) + high_ref[...].astype(FULL)).astype(LOW)


def rows_of(ref, at, count):
    return ref[pl.ds(pl.multiple_of(at * count, count), count), :]


def halve_kernel(bit_ref, kept_ref, came_ref, send_ref, keep_ref):
    half = kept_ref.shape[0] // 2
    bit = bit_ref[0]
    keep_ref[...] = rows_of(kept_ref, bit, half) + rows_of(came_ref, bit, half).astype(FULL)
    send_ref[...] = (rows_of(kept_ref, 1 - bit, half) + rows_of(came_ref, 1 - bit, half).astype(FULL)).astype(LOW)


def add_kernel(*refs):
    total = refs[0][...].astype(FULL)
    for ref in refs[1:-1]:
        total = total + ref[...].astype(FULL)
    refs[-1][...] = total.astype(LOW)


def joined_kernel(bit_ref, own_ref, came_ref, term_a_ref, term_b_ref, out_ref):
    size = own_ref.shape[0]
    bit = bit_ref[0]
    out_ref[pl.ds(pl.multiple_of(bit * size, size), size), :] = own_ref[...]
    out_ref[pl.ds(pl.multiple_of((1 - bit) * size, size), size), :] = came_ref[...]
    out_ref[2 * size :, :] = (term_a_ref[...].astype(FULL) + term_b_ref[...].astype(FULL)).astype(LOW)


def total_of(squares_of):
    return jnp.sum(jnp.sum(squares_of * squares_of, axis=0, keepdims=True), axis=1, keepdims=True)


def scale_kernel(channels, bit_ref, own_ref, came_ref, *refs):
    out_refs, both_ref = refs[:5], refs[5]
    bound = math.sqrt(5.0) * channels
    squares = total_of(own_ref[...].astype(FULL)) + total_of(came_ref[...].astype(FULL))
    factor = bound / jnp.maximum(jnp.sqrt(squares), bound)
    both_ref[bit_ref[0]] = own_ref[...]
    both_ref[1 - bit_ref[0]] = came_ref[...]
    half = channels // 2
    for h in range(2):
        for t in range(2):
            out_refs[1 + 2 * h + t][...] = both_ref[h, t * channels : (t + 1) * channels, :].astype(FULL) * factor
        out_refs[0][h * half : (h + 1) * half, :] = both_ref[h, 2 * channels :, :].astype(FULL) * factor


def on_device(cell_feats, neighbours, member_cell, member_jet, cotangent, message_weight, query_weight, key_weight, value_weight, output_weight):
    events, per_device, channels = cell_feats.shape
    assert events == 1
    members_dev = member_cell.shape[1]
    plan = Plan(lax.axis_size("phi"), per_device, members_dev, channels)
    window, chunk = plan.window, plan.chunk
    place = lax.axis_index("phi").astype(jnp.int32).reshape(1)
    cells, cot, nbrs = cell_feats[0], cotangent[0], neighbours[0]
    low = shifted(cells[per_device - BLOCK :], "phi", 1)
    high = shifted(cells[:BLOCK], "phi", -1)
    total = window * chunk
    lines = -(-plan.blocks * (plan.blocks + 2) // 8) * 8
    pick, put, times, *cot_chunks = call(
        lambda *refs: index_kernel(plan, *refs),
        [((total, per_device), LOW), ((per_device, total), LOW), ((lines, channels), FULL)]
        + [((chunk, channels), LOW)] * window,
        [place, nbrs],
        [member_cell.reshape(1, members_dev), member_jet.reshape(1, members_dev), cot],
        micros=0.5,
    )
    gathered, before, hidden, *chunks = call(
        lambda *refs: hidden_kernel(plan, *refs),
        [((per_device, channels), LOW), ((per_device, channels), FULL), ((per_device, channels), LOW)]
        + [((2 * chunk, channels), LOW)] * window,
        [],
        [times, cells, low, high, message_weight, pick, *cot_chunks],
        micros=1.0,
    )

    chunks = plan.routed(chunks)
    weights = [query_weight, key_weight, value_weight, output_weight]
    (parts,) = call(
        lambda *refs: attend_kernel(plan, *refs), [((6, plan.owned, channels), LOW)], [], [*chunks, *weights], micros=2.5
    )
    backs = call(
        lambda *refs: back_kernel(plan, *refs),
        [((2 * chunk, channels), LOW)] * window,
        [],
        [parts, *weights],
        micros=0.7,
    )
    backs = plan.routed(backs, back=True)
    core, across = [((lax.axis_index("ev") >> b) & 1).astype(jnp.int32).reshape(1) for b in range(2)]
    a_send, a_keep = call(
        lambda *refs: term_kernel(channels, *refs),
        [((2 * channels, channels), LOW), ((2 * channels, channels), FULL)],
        [core],
        [parts],
    )
    a_came = swapped(a_send, "ev", 1)
    a_send, a_keep = call(halve_kernel, [((channels, channels), LOW), ((channels, channels), FULL)], [across], [a_keep, a_came])
    a_came = swapped(a_send, "ev", 2)
    half = channels // 2
    out_cells, kept, first, last, m_send, m_keep = call(
        lambda *refs: return_kernel(plan, *refs),
        [
            ((per_device, channels), LOW),
            ((per_device, channels), FULL),
            ((BLOCK, channels), LOW),
            ((BLOCK, channels), LOW),
            ((half, channels), LOW),
            ((half, channels), FULL),
        ],
        [core],
        [times, *backs, put, hidden, cot, before, gathered, message_weight],
        [pltpu.VMEM((2, total, channels), LOW), pltpu.VMEM((2, half, channels), FULL)],
        micros=4.0,
    )
    def added(rows, *parts):
        return call(add_kernel, [((rows, channels), LOW)], [], list(parts))[0]

    m_came = swapped(m_send, "ev", 1)
    a_own = added(channels, a_keep, a_came)
    from_lower = shifted(last, "phi", 1)
    from_upper = shifted(first, "phi", -1)
    m_own = added(half, m_keep, m_came)
    m_came = swapped(m_own, "ev", 2)
    mask = 1
    while mask < plan.sectors:
        a_came = swapped(a_own, "phi", mask)
        m_own = added(half, m_own, m_came)
        if 2 * mask == plan.sectors:
            m_own = lax.optimization_barrier((m_own, from_lower, from_upper))[0]
        m_came = swapped(m_own, "phi", mask)
        a_own = added(channels, a_own, a_came)
        mask *= 2
    a_came = swapped(a_own, "ev", 2)
    (grad_cells,) = call(
        lambda *refs: edges_kernel(plan, *refs), [((per_device, channels), LOW)], [], [kept, from_lower, from_upper]
    )
    m_came, grad_cells = lax.optimization_barrier((m_came, grad_cells))
    (own,) = call(joined_kernel, [((2 * channels + half, channels), LOW)], [across], [a_own, a_came, m_own, m_came])
    came = swapped(own, "ev", 1)
    grads = call(
        lambda *refs: scale_kernel(channels, *refs),
        [((channels, channels), FULL)] * 5,
        [core],
        [own, came],
        [pltpu.VMEM((2, 2 * channels + half, channels), LOW)],
        final=True,
    )
    return (out_cells[None], grad_cells[None], *grads)


def solution(mesh):
    cells = P(("groups", "ev"), "phi", None)
    flat = P(("groups", "ev"), "phi")
    weights = P("groups", None)
    return jax.shard_map(
        on_device,
        mesh=mesh,
        in_specs=(cells, cells, flat, cells, cells, P(), P(), P(), P(), P()),
        out_specs=(cells, cells, weights, weights, weights, weights, weights),
        check_vma=False,
    )
```

```python
import math

import jax
import jax.numpy as jnp
from jax import lax
from jax.experimental import pallas as pl
from jax.experimental.pallas import tpu as pltpu
from jax.sharding import PartitionSpec as P

HEADS = 8
BLOCK = 128
NBRS = 4
JET_DEV = 4
LOW = jnp.bfloat16
FULL = jnp.float32
VMEM = pl.BlockSpec(memory_space=pltpu.VMEM)
SMEM = pl.BlockSpec(memory_space=pltpu.SMEM)


def call(body, outs, scalars, arrays, scratch=(), final=False, micros=0.1):
    kind = jax.ShapeDtypeStruct if final else pltpu.VMEM
    return pl.pallas_call(
        body,
        out_shape=[kind(shape, dtype) for shape, dtype in outs],
        in_specs=[SMEM] * len(scalars) + [VMEM] * len(arrays),
        out_specs=[VMEM] * len(outs),
        scratch_shapes=list(scratch),
        compiler_params=pltpu.CompilerParams(vmem_limit_bytes=16 << 20),
        cost_estimate=pl.CostEstimate(flops=int(micros * 1e9), transcendentals=0, bytes_accessed=0),
    )(*scalars, *[pltpu.with_memory_space_constraint(x, pltpu.VMEM) for x in arrays])


def shifted(block, axis, distance):
    count = lax.axis_size(axis)
    return lax.ppermute(block, axis, [((i - distance) % count, i) for i in range(count)])


def swapped(block, axis, mask):
    return lax.ppermute(block, axis, [(i, i ^ mask) for i in range(lax.axis_size(axis))])


def mm(a, b):
    return lax.dot_general(a, b, (((1,), (0,)), ((), ())), preferred_element_type=FULL)


def mm_nt(a, b):
    return lax.dot_general(a, b, (((1,), (1,)), ((), ())), preferred_element_type=FULL)


def mm_tn(a, b):
    return lax.dot_general(a, b, (((0,), (0,)), ((), ())), preferred_element_type=FULL)


def iota(shape, dim):
    return lax.broadcasted_iota(jnp.int32, shape, dim)


class Plan:
    def __init__(self, sectors, per_device, members_dev, channels):
        self.sectors, self.cells, self.members, self.channels = sectors, per_device, members_dev, channels
        self.blocks = per_device // BLOCK
        self.radius = min(4, (sectors - 1) // 2)
        self.window = 2 * self.radius + 1
        self.cap = max(2, 2 * members_dev // (JET_DEV * self.window))
        self.used = JET_DEV * self.cap
        self.chunk = -(-(self.used + 1) // 8) * 8
        self.slots = -(-self.window * self.cap // 64) * 64
        self.owned = JET_DEV * self.slots
        assert sectors % 2 == 0
        self.hops = sorted((o ^ 1 for o in range(-self.radius, self.radius + 1)), key=lambda hop: (hop != 0, -abs(hop)))

    def seat(self, c, w):
        jet = sum((c >= t * self.cap).astype(jnp.int32) for t in range(1, JET_DEV))
        return jnp.where(c < self.used, c + jet * (self.slots - self.cap) + w * self.cap, -1)

    def routed(self, parts, back=False):
        n = self.sectors
        moved = []
        for part, hop in zip(parts, self.hops):
            route = [(p, (p + (hop if p % 2 == 0 else -hop)) % n) for p in range(n)]
            if back:
                route = [(there, here) for here, there in route]
            moved.append(lax.ppermute(part, "phi", route) if hop else part)
        return moved


def index_kernel(plan, where_ref, nbr_ref, cell_ref, jet_ref, cot_ref, pick_ref, place_ref, times_ref, *chunk_refs):
    sector = where_ref[0]
    entries = plan.blocks + 2
    line = iota(times_ref.shape, 0)
    times = jnp.zeros(times_ref.shape, FULL)
    for b in range(plan.blocks):
        for j in range(entries):
            share = sum((nbr_ref[b, k] == j).astype(FULL) for k in range(NBRS)) * (1.0 / NBRS)
            times = jnp.where(line == b * entries + j, share, times)
    times_ref[...] = times
    count, members = plan.chunk, plan.members
    jets = jet_ref[...]
    hop = lax.bitwise_xor(lax.shift_right_logical(jets, 2), 1) - sector
    hop = jnp.where(lax.bitwise_and(sector, 1) == 0, hop, -hop)
    hop = jnp.where(hop < 0, hop + plan.sectors, hop)
    offset = sum(jnp.where(hop == known % plan.sectors, k, 0) for k, known in enumerate(plan.hops))
    inner = lax.bitwise_and(jets, 3)
    row = (offset * JET_DEV + inner).astype(FULL)
    rows, cols = iota((members, members), 0), iota((members, members), 1)
    column = jnp.sum(jnp.where(rows == cols, row, 0.0), axis=1, keepdims=True)
    earlier = jnp.where((column == row) & (rows < cols), 1.0, 0.0)
    rank = jnp.sum(earlier, axis=0, keepdims=True)
    target = offset * count + inner * plan.cap + rank.astype(jnp.int32)
    total = plan.window * count
    slot_hot = jnp.where(iota((total, members), 0) == target, 1.0, 0.0).astype(LOW)
    cell_hot = jnp.where(iota((plan.cells, members), 0) == cell_ref[...], 1.0, 0.0).astype(LOW)
    pick = mm_nt(slot_hot, cell_hot).astype(LOW)
    pick_ref[...] = pick
    place_ref[...] = mm_nt(cell_hot, slot_hot).astype(LOW)
    ones = jnp.ones((8, members), LOW)
    wide = iota((plan.channels, members), 0)
    mask_row = iota((count, plan.channels), 0) == plan.used
    chosen = mm(pick, cot_ref[...])
    for w in range(plan.window):
        hot = jnp.where((wide + w * count == target) & (wide < count), 1.0, 0.0).astype(LOW)
        present = mm_nt(ones, hot)[0:1, :]
        part = chosen[w * count : (w + 1) * count, :]
        chunk_refs[w][...] = jnp.where(mask_row, present, part).astype(LOW)


def hidden_kernel(plan, times_ref, cell_ref, low_ref, high_ref, weight_ref, pick_ref, *refs):
    blocks = plan.blocks
    cot_refs, chunk_refs = refs[: plan.window], refs[plan.window + 3 :]
    gathered_ref, before_ref, hidden_ref = refs[plan.window : plan.window + 3]
    entries = [low_ref[...].astype(FULL)]
    entries += [cell_ref[b * BLOCK : (b + 1) * BLOCK, :].astype(FULL) for b in range(blocks)]
    entries += [high_ref[...].astype(FULL)]
    for b in range(blocks):
        total = None
        for j, entry in enumerate(entries):
            line = b * len(entries) + j
            part = entry * times_ref[line : line + 1, :]
            total = part if total is None else total + part
        gathered_ref[b * BLOCK : (b + 1) * BLOCK, :] = total.astype(LOW)
    before = mm(gathered_ref[...], weight_ref[...])
    before_ref[...] = before
    silu = before * (1.0 / (1.0 + jnp.exp(-before)))
    hidden = (cell_ref[...].astype(FULL) + silu).astype(LOW)
    hidden_ref[...] = hidden
    chosen = mm(pick_ref[...], hidden).astype(LOW)
    for w in range(plan.window):
        chunk_refs[w][: plan.chunk, :] = chosen[w * plan.chunk : (w + 1) * plan.chunk, :]
        chunk_refs[w][plan.chunk :, :] = cot_refs[w][...]


def attend_kernel(plan, *refs):
    window, count, slots, owned, channels = plan.window, plan.chunk, plan.slots, plan.owned, plan.channels
    chunk_refs = refs[:window]
    wq_ref, wk_ref, wv_ref, wo_ref, parts_ref = refs[window:]
    head = channels // HEADS
    scale = 1.0 / math.sqrt(head)

    members = upstream = present = None
    base = plan.used // 8 * 8
    for w in range(window):
        hot = jnp.where(iota((owned, count), 0) == plan.seat(iota((owned, count), 1), w), 1.0, 0.0)
        low = hot.astype(LOW)
        m, u = mm(low, chunk_refs[w][:count, :]), mm(low, chunk_refs[w][count:, :])
        tail = chunk_refs[w][count + base : count + base + 8, :].astype(FULL)
        row = jnp.sum(jnp.where(iota(tail.shape, 0) == plan.used - base, tail, 0.0), axis=0, keepdims=True)
        p = jnp.sum(hot * row[:, :count], axis=1, keepdims=True)
        members = m if members is None else members + m
        upstream = u if upstream is None else upstream + u
        present = p if present is None else present + p
    members, upstream = members.astype(LOW), upstream.astype(LOW)
    queries = mm(members, wq_ref[...]).astype(LOW)
    keys = mm(members, wk_ref[...]).astype(LOW)
    vals = mm(members, wv_ref[...]).astype(LOW)
    grad_mix = mm_nt(upstream, wo_ref[...]).astype(LOW)
    lane = iota((1, channels), 1)
    head_of = [(lane >= h * head) & (lane < (h + 1) * head) for h in range(HEADS)]
    low_of = [jnp.where(h, 1.0, 0.0).astype(LOW) for h in head_of]

    def spread(block):
        return jnp.concatenate([block * low_of[h] for h in range(HEADS)], axis=0)

    def merged(wide):
        total = None
        for h in range(HEADS):
            part = jnp.where(head_of[h], wide[h * slots : (h + 1) * slots, :], 0.0)
            total = part if total is None else total + part
        return total

    jets = range(JET_DEV)
    spans = [slice(j * slots, (j + 1) * slots) for j in jets]
    q_wide, g_wide = [spread(queries[x]) for x in spans], [spread(grad_mix[x]) for x in spans]
    scores = [mm_nt(keys[x], wide) for x, wide in zip(spans, q_wide)]
    grad_chances = [mm_nt(vals[x], wide) for x, wide in zip(spans, g_wide)]
    chances_low, grad_scores = [], []
    for j in jets:
        masked = jnp.where(present[spans[j]] > 0.5, scores[j] * scale, -1e30)
        powers = jnp.exp(masked - jnp.max(masked, axis=0, keepdims=True))
        chances = powers * (1.0 / jnp.sum(powers, axis=0, keepdims=True))
        chances_low.append(chances.astype(LOW))
        inner = jnp.sum(chances * grad_chances[j], axis=0, keepdims=True)
        grad_scores.append((chances * (grad_chances[j] - inner) * scale).astype(LOW))
    grad_k = [mm(grad_scores[j], q_wide[j]).astype(LOW) for j in jets]
    grad_v = [mm(chances_low[j], g_wide[j]).astype(LOW) for j in jets]

    def turned(wide):
        tall = wide.T
        return jnp.concatenate([tall[h * slots : (h + 1) * slots, :] for h in range(HEADS)], axis=1)

    mixture = [mm(turned(chances_low[j]), spread(vals[spans[j]])).astype(LOW) for j in jets]
    grad_q = [mm(turned(grad_scores[j]), spread(keys[spans[j]])).astype(LOW) for j in jets]
    mixture, grad_q, grad_k, grad_v = [jnp.concatenate(x, axis=0) for x in (mixture, grad_q, grad_k, grad_v)]
    parts_ref[0] = members
    parts_ref[1] = upstream
    parts_ref[2] = mixture
    parts_ref[3] = grad_q
    parts_ref[4] = grad_k
    parts_ref[5] = grad_v


def back_kernel(plan, parts_ref, wq_ref, wk_ref, wv_ref, wo_ref, *back_refs):
    count, owned = plan.chunk, plan.owned
    attended = mm(parts_ref[2], wo_ref[...]).astype(LOW)
    grad_members = mm_nt(parts_ref[3], wq_ref[...]) + mm_nt(parts_ref[4], wk_ref[...]) + mm_nt(parts_ref[5], wv_ref[...])
    grad_members = grad_members.astype(LOW)
    for w in range(plan.window):
        hot = jnp.where(plan.seat(iota((count, owned), 0), w) == iota((count, owned), 1), 1.0, 0.0).astype(LOW)
        back_refs[w][:count, :] = mm(hot, attended).astype(LOW)
        back_refs[w][count:, :] = mm(hot, grad_members).astype(LOW)


def term_kernel(channels, bit_ref, parts_ref, send_ref, keep_ref):
    bit = bit_ref[0]
    for half, ref in ((1 - bit, send_ref), (bit, keep_ref)):
        for t in range(2):
            term = 2 * half + t
            left = parts_ref[jnp.where(term == 3, 2, 0)]
            right = parts_ref[jnp.where(term == 3, 1, 3 + term)]
            ref[t * channels : (t + 1) * channels, :] = mm_tn(left, right).astype(ref.dtype)


def return_kernel(plan, bit_ref, times_ref, *refs):
    window, count = plan.window, plan.chunk
    back_refs = refs[:window]
    place_ref, hidden_ref, cot_ref, before_ref, gathered_ref, weight_ref = refs[window : window + 6]
    out_ref, kept_ref, first_ref, last_ref, send_ref, keep_ref, rows_ref, term_ref = refs[window + 6 :]
    place = place_ref[...]
    for w in range(window):
        rows_ref[0, w * count : (w + 1) * count, :] = back_refs[w][:count, :]
        rows_ref[1, w * count : (w + 1) * count, :] = back_refs[w][count:, :]
    out_ref[...] = (hidden_ref[...].astype(FULL) + mm(place, rows_ref[0])).astype(LOW)
    grad_hidden = cot_ref[...].astype(FULL) + mm(place, rows_ref[1])
    before = before_ref[...]
    sigmoid = 1.0 / (1.0 + jnp.exp(-before))
    slope = sigmoid * (1.0 + before * (1.0 - sigmoid))
    grad_before = (grad_hidden * slope).astype(LOW)
    grad_gathered = mm_nt(grad_before, weight_ref[...]).astype(LOW).astype(FULL)

    def extended(j):
        total = None
        for b in range(plan.blocks):
            line = b * (plan.blocks + 2) + j
            part = grad_gathered[b * BLOCK : (b + 1) * BLOCK, :] * times_ref[line : line + 1, :]
            total = part if total is None else total + part
        return total.astype(LOW)

    first_ref[...] = extended(0)
    last_ref[...] = extended(plan.blocks + 1)
    for b in range(plan.blocks):
        span = slice(b * BLOCK, (b + 1) * BLOCK)
        kept_ref[span, :] = grad_hidden[span] + extended(b + 1).astype(FULL)
    half = plan.channels // 2
    term_ref[...] = mm_tn(gathered_ref[...], grad_before).reshape(2, half, plan.channels)
    send_ref[...] = term_ref[1 - bit_ref[0]].astype(LOW)
    keep_ref[...] = term_ref[bit_ref[0]]


def edges_kernel(plan, kept_ref, low_ref, high_ref, out_ref):
    last = plan.cells - BLOCK
    if last:
        out_ref[:BLOCK, :] = (kept_ref[:BLOCK, :] + low_ref[...].astype(FULL)).astype(LOW)
        if last > BLOCK:
            out_ref[BLOCK:last, :] = kept_ref[BLOCK:last, :].astype(LOW)
        out_ref[last:, :] = (kept_ref[last:, :] + high_ref[...].astype(FULL)).astype(LOW)
    else:
        out_ref[...] = (kept_ref[...] + low_ref[...].astype(FULL) + high_ref[...].astype(FULL)).astype(LOW)


def rows_of(ref, at, count):
    return ref[pl.ds(pl.multiple_of(at * count, count), count), :]


def halve_kernel(bit_ref, kept_ref, came_ref, send_ref, keep_ref):
    half = kept_ref.shape[0] // 2
    bit = bit_ref[0]
    keep_ref[...] = rows_of(kept_ref, bit, half) + rows_of(came_ref, bit, half).astype(FULL)
    send_ref[...] = (rows_of(kept_ref, 1 - bit, half) + rows_of(came_ref, 1 - bit, half).astype(FULL)).astype(LOW)


def add_kernel(*refs):
    total = refs[0][...].astype(FULL)
    for ref in refs[1:-1]:
        total = total + ref[...].astype(FULL)
    refs[-1][...] = total.astype(LOW)


def joined_kernel(bit_ref, own_ref, came_ref, term_a_ref, term_b_ref, out_ref):
    size = own_ref.shape[0]
    bit = bit_ref[0]
    out_ref[pl.ds(pl.multiple_of(bit * size, size), size), :] = own_ref[...]
    out_ref[pl.ds(pl.multiple_of((1 - bit) * size, size), size), :] = came_ref[...]
    out_ref[2 * size :, :] = (term_a_ref[...].astype(FULL) + term_b_ref[...].astype(FULL)).astype(LOW)


def total_of(squares_of):
    return jnp.sum(jnp.sum(squares_of * squares_of, axis=0, keepdims=True), axis=1, keepdims=True)


def scale_kernel(channels, bit_ref, own_ref, came_ref, *refs):
    out_refs, both_ref = refs[:5], refs[5]
    bound = math.sqrt(5.0) * channels
    squares = total_of(own_ref[...].astype(FULL)) + total_of(came_ref[...].astype(FULL))
    factor = bound / jnp.maximum(jnp.sqrt(squares), bound)
    both_ref[bit_ref[0]] = own_ref[...]
    both_ref[1 - bit_ref[0]] = came_ref[...]
    half = channels // 2
    for h in range(2):
        for t in range(2):
            out_refs[1 + 2 * h + t][...] = both_ref[h, t * channels : (t + 1) * channels, :].astype(FULL) * factor
        out_refs[0][h * half : (h + 1) * half, :] = both_ref[h, 2 * channels :, :].astype(FULL) * factor


def on_device(cell_feats, neighbours, member_cell, member_jet, cotangent, message_weight, query_weight, key_weight, value_weight, output_weight):
    events, per_device, channels = cell_feats.shape
    assert events == 1
    members_dev = member_cell.shape[1]
    plan = Plan(lax.axis_size("phi"), per_device, members_dev, channels)
    window, chunk = plan.window, plan.chunk
    place = lax.axis_index("phi").astype(jnp.int32).reshape(1)
    cells, cot, nbrs = cell_feats[0], cotangent[0], neighbours[0]
    low = shifted(cells[per_device - BLOCK :], "phi", 1)
    high = shifted(cells[:BLOCK], "phi", -1)
    total = window * chunk
    lines = -(-plan.blocks * (plan.blocks + 2) // 8) * 8
    pick, put, times, *cot_chunks = call(
        lambda *refs: index_kernel(plan, *refs),
        [((total, per_device), LOW), ((per_device, total), LOW), ((lines, channels), FULL)]
        + [((chunk, channels), LOW)] * window,
        [place, nbrs],
        [member_cell.reshape(1, members_dev), member_jet.reshape(1, members_dev), cot],
        micros=0.5,
    )
    gathered, before, hidden, *chunks = call(
        lambda *refs: hidden_kernel(plan, *refs),
        [((per_device, channels), LOW), ((per_device, channels), FULL), ((per_device, channels), LOW)]
        + [((2 * chunk, channels), LOW)] * window,
        [],
        [times, cells, low, high, message_weight, pick, *cot_chunks],
        micros=1.0,
    )

    chunks = plan.routed(chunks)
    weights = [query_weight, key_weight, value_weight, output_weight]
    (parts,) = call(
        lambda *refs: attend_kernel(plan, *refs), [((6, plan.owned, channels), LOW)], [], [*chunks, *weights], micros=2.5
    )
    backs = call(
        lambda *refs: back_kernel(plan, *refs),
        [((2 * chunk, channels), LOW)] * window,
        [],
        [parts, *weights],
        micros=0.7,
    )
    core, across = [((lax.axis_index("ev") >> b) & 1).astype(jnp.int32).reshape(1) for b in range(2)]
    a_send, a_keep = call(
        lambda *refs: term_kernel(channels, *refs),
        [((2 * channels, channels), LOW), ((2 * channels, channels), FULL)],
        [core],
        [parts],
    )
    a_came = swapped(a_send, "ev", 1)
    a_came = lax.optimization_barrier((a_came, *backs))[0]
    backs = plan.routed(backs, back=True)
    a_send, a_keep = call(halve_kernel, [((channels, channels), LOW), ((channels, channels), FULL)], [across], [a_keep, a_came])
    a_came = swapped(a_send, "ev", 2)
    half = channels // 2
    out_cells, kept, first, last, m_send, m_keep = call(
        lambda *refs: return_kernel(plan, *refs),
        [
            ((per_device, channels), LOW),
            ((per_device, channels), FULL),
            ((BLOCK, channels), LOW),
            ((BLOCK, channels), LOW),
            ((half, channels), LOW),
            ((half, channels), FULL),
        ],
        [core],
        [times, *backs, put, hidden, cot, before, gathered, message_weight],
        [pltpu.VMEM((2, total, channels), LOW), pltpu.VMEM((2, half, channels), FULL)],
        micros=4.0,
    )
    def added(rows, *parts):
        return call(add_kernel, [((rows, channels), LOW)], [], list(parts))[0]

    m_came = swapped(m_send, "ev", 1)
    a_own = added(channels, a_keep, a_came)
    from_lower = shifted(last, "phi", 1)
    from_upper = shifted(first, "phi", -1)
    m_own = added(half, m_keep, m_came)
    m_came = swapped(m_own, "ev", 2)
    mask = 1
    while mask < plan.sectors:
        a_came = swapped(a_own, "phi", mask)
        if mask == 1:
            a_came = lax.optimization_barrier((a_came, m_own))[0]
        m_own = added(half, m_own, m_came)
        m_came = swapped(m_own, "phi", mask)
        a_own = added(channels, a_own, a_came)
        mask *= 2
    a_own = lax.optimization_barrier((a_own, from_lower, from_upper))[0]
    a_came = swapped(a_own, "ev", 2)
    (grad_cells,) = call(
        lambda *refs: edges_kernel(plan, *refs), [((per_device, channels), LOW)], [], [kept, from_lower, from_upper]
    )
    m_came, grad_cells = lax.optimization_barrier((m_came, grad_cells))
    (own,) = call(joined_kernel, [((2 * channels + half, channels), LOW)], [across], [a_own, a_came, m_own, m_came])
    came = swapped(own, "ev", 1)
    grads = call(
        lambda *refs: scale_kernel(channels, *refs),
        [((channels, channels), FULL)] * 5,
        [core],
        [own, came],
        [pltpu.VMEM((2, 2 * channels + half, channels), LOW)],
        final=True,
    )
    return (out_cells[None], grad_cells[None], *grads)


def solution(mesh):
    cells = P(("groups", "ev"), "phi", None)
    flat = P(("groups", "ev"), "phi")
    weights = P("groups", None)
    return jax.shard_map(
        on_device,
        mesh=mesh,
        in_specs=(cells, cells, flat, cells, cells, P(), P(), P(), P(), P()),
        out_specs=(cells, cells, weights, weights, weights, weights, weights),
        check_vma=False,
    )
```

```python
import math

import jax
import jax.numpy as jnp
from jax import lax
from jax.experimental import pallas as pl
from jax.experimental.pallas import tpu as pltpu
from jax.sharding import PartitionSpec as P

HEADS = 8
BLOCK = 128
NBRS = 4
JET_DEV = 4
LOW = jnp.bfloat16
FULL = jnp.float32
VMEM = pl.BlockSpec(memory_space=pltpu.VMEM)
SMEM = pl.BlockSpec(memory_space=pltpu.SMEM)


def call(body, outs, scalars, arrays, scratch=(), final=False, micros=0.1):
    kind = jax.ShapeDtypeStruct if final else pltpu.VMEM
    return pl.pallas_call(
        body,
        out_shape=[kind(shape, dtype) for shape, dtype in outs],
        in_specs=[SMEM] * len(scalars) + [VMEM] * len(arrays),
        out_specs=[VMEM] * len(outs),
        scratch_shapes=list(scratch),
        compiler_params=pltpu.CompilerParams(vmem_limit_bytes=16 << 20),
        cost_estimate=pl.CostEstimate(flops=int(micros * 1e9), transcendentals=0, bytes_accessed=0),
    )(*scalars, *[pltpu.with_memory_space_constraint(x, pltpu.VMEM) for x in arrays])


def shifted(block, axis, distance):
    count = lax.axis_size(axis)
    return lax.ppermute(block, axis, [((i - distance) % count, i) for i in range(count)])


def swapped(block, axis, mask):
    return lax.ppermute(block, axis, [(i, i ^ mask) for i in range(lax.axis_size(axis))])


def mm(a, b):
    return lax.dot_general(a, b, (((1,), (0,)), ((), ())), preferred_element_type=FULL)


def mm_nt(a, b):
    return lax.dot_general(a, b, (((1,), (1,)), ((), ())), preferred_element_type=FULL)


def mm_tn(a, b):
    return lax.dot_general(a, b, (((0,), (0,)), ((), ())), preferred_element_type=FULL)


def iota(shape, dim):
    return lax.broadcasted_iota(jnp.int32, shape, dim)


class Plan:
    def __init__(self, sectors, per_device, members_dev, channels):
        self.sectors, self.cells, self.members, self.channels = sectors, per_device, members_dev, channels
        self.blocks = per_device // BLOCK
        self.radius = min(4, (sectors - 1) // 2)
        self.window = 2 * self.radius + 1
        self.cap = max(2, 2 * members_dev // (JET_DEV * self.window))
        self.used = JET_DEV * self.cap
        self.chunk = -(-(self.used + 1) // 8) * 8
        self.slots = -(-self.window * self.cap // 64) * 64
        self.owned = JET_DEV * self.slots
        assert sectors % 2 == 0
        self.hops = sorted((o ^ 1 for o in range(-self.radius, self.radius + 1)), key=lambda hop: (hop != 0, -abs(hop)))

    def seat(self, c, w):
        jet = sum((c >= t * self.cap).astype(jnp.int32) for t in range(1, JET_DEV))
        return jnp.where(c < self.used, c + jet * (self.slots - self.cap) + w * self.cap, -1)

    def routed(self, parts, back=False):
        n = self.sectors
        moved = []
        for part, hop in zip(parts, self.hops):
            route = [(p, (p + (hop if p % 2 == 0 else -hop)) % n) for p in range(n)]
            if back:
                route = [(there, here) for here, there in route]
            moved.append(lax.ppermute(part, "phi", route) if hop else part)
        return moved


def index_kernel(plan, where_ref, nbr_ref, cell_ref, jet_ref, cot_ref, pick_ref, place_ref, times_ref, *chunk_refs):
    sector = where_ref[0]
    entries = plan.blocks + 2
    line = iota(times_ref.shape, 0)
    times = jnp.zeros(times_ref.shape, FULL)
    for b in range(plan.blocks):
        for j in range(entries):
            share = sum((nbr_ref[b, k] == j).astype(FULL) for k in range(NBRS)) * (1.0 / NBRS)
            times = jnp.where(line == b * entries + j, share, times)
    times_ref[...] = times
    count, members = plan.chunk, plan.members
    jets = jet_ref[...]
    hop = lax.bitwise_xor(lax.shift_right_logical(jets, 2), 1) - sector
    hop = jnp.where(lax.bitwise_and(sector, 1) == 0, hop, -hop)
    hop = jnp.where(hop < 0, hop + plan.sectors, hop)
    offset = sum(jnp.where(hop == known % plan.sectors, k, 0) for k, known in enumerate(plan.hops))
    inner = lax.bitwise_and(jets, 3)
    row = (offset * JET_DEV + inner).astype(FULL)
    rows, cols = iota((members, members), 0), iota((members, members), 1)
    column = jnp.sum(jnp.where(rows == cols, row, 0.0), axis=1, keepdims=True)
    earlier = jnp.where((column == row) & (rows < cols), 1.0, 0.0)
    rank = jnp.sum(earlier, axis=0, keepdims=True)
    target = offset * count + inner * plan.cap + rank.astype(jnp.int32)
    total = plan.window * count
    slot_hot = jnp.where(iota((total, members), 0) == target, 1.0, 0.0).astype(LOW)
    cell_hot = jnp.where(iota((plan.cells, members), 0) == cell_ref[...], 1.0, 0.0).astype(LOW)
    pick = mm_nt(slot_hot, cell_hot).astype(LOW)
    pick_ref[...] = pick
    place_ref[...] = mm_nt(cell_hot, slot_hot).astype(LOW)
    ones = jnp.ones((8, members), LOW)
    wide = iota((plan.channels, members), 0)
    mask_row = iota((count, plan.channels), 0) == plan.used
    chosen = mm(pick, cot_ref[...])
    for w in range(plan.window):
        hot = jnp.where((wide + w * count == target) & (wide < count), 1.0, 0.0).astype(LOW)
        present = mm_nt(ones, hot)[0:1, :]
        part = chosen[w * count : (w + 1) * count, :]
        chunk_refs[w][...] = jnp.where(mask_row, present, part).astype(LOW)


def hidden_kernel(plan, times_ref, cell_ref, low_ref, high_ref, weight_ref, pick_ref, *refs):
    blocks = plan.blocks
    cot_refs, chunk_refs = refs[: plan.window], refs[plan.window + 3 :]
    gathered_ref, before_ref, hidden_ref = refs[plan.window : plan.window + 3]
    entries = [low_ref[...].astype(FULL)]
    entries += [cell_ref[b * BLOCK : (b + 1) * BLOCK, :].astype(FULL) for b in range(blocks)]
    entries += [high_ref[...].astype(FULL)]
    for b in range(blocks):
        total = None
        for j, entry in enumerate(entries):
            line = b * len(entries) + j
            part = entry * times_ref[line : line + 1, :]
            total = part if total is None else total + part
        gathered_ref[b * BLOCK : (b + 1) * BLOCK, :] = total.astype(LOW)
    before = mm(gathered_ref[...], weight_ref[...])
    before_ref[...] = before
    silu = before * (1.0 / (1.0 + jnp.exp(-before)))
    hidden = (cell_ref[...].astype(FULL) + silu).astype(LOW)
    hidden_ref[...] = hidden
    chosen = mm(pick_ref[...], hidden).astype(LOW)
    for w in range(plan.window):
        chunk_refs[w][: plan.chunk, :] = chosen[w * plan.chunk : (w + 1) * plan.chunk, :]
        chunk_refs[w][plan.chunk :, :] = cot_refs[w][...]


def attend_kernel(plan, bit_ref, *refs):
    window, count, slots, owned, channels = plan.window, plan.chunk, plan.slots, plan.owned, plan.channels
    chunk_refs = refs[:window]
    wq_ref, wk_ref, wv_ref, wo_ref, parts_ref, send_ref, keep_ref = refs[window:]
    head = channels // HEADS
    scale = 1.0 / math.sqrt(head)

    members = upstream = present = None
    base = plan.used // 8 * 8
    for w in range(window):
        hot = jnp.where(iota((owned, count), 0) == plan.seat(iota((owned, count), 1), w), 1.0, 0.0)
        low = hot.astype(LOW)
        m, u = mm(low, chunk_refs[w][:count, :]), mm(low, chunk_refs[w][count:, :])
        tail = chunk_refs[w][count + base : count + base + 8, :].astype(FULL)
        row = jnp.sum(jnp.where(iota(tail.shape, 0) == plan.used - base, tail, 0.0), axis=0, keepdims=True)
        p = jnp.sum(hot * row[:, :count], axis=1, keepdims=True)
        members = m if members is None else members + m
        upstream = u if upstream is None else upstream + u
        present = p if present is None else present + p
    members, upstream = members.astype(LOW), upstream.astype(LOW)
    queries = mm(members, wq_ref[...]).astype(LOW)
    keys = mm(members, wk_ref[...]).astype(LOW)
    vals = mm(members, wv_ref[...]).astype(LOW)
    grad_mix = mm_nt(upstream, wo_ref[...]).astype(LOW)
    lane = iota((1, channels), 1)
    head_of = [(lane >= h * head) & (lane < (h + 1) * head) for h in range(HEADS)]
    low_of = [jnp.where(h, 1.0, 0.0).astype(LOW) for h in head_of]

    def spread(block):
        return jnp.concatenate([block * low_of[h] for h in range(HEADS)], axis=0)

    def merged(wide):
        total = None
        for h in range(HEADS):
            part = jnp.where(head_of[h], wide[h * slots : (h + 1) * slots, :], 0.0)
            total = part if total is None else total + part
        return total

    jets = range(JET_DEV)
    spans = [slice(j * slots, (j + 1) * slots) for j in jets]
    q_wide, g_wide = [spread(queries[x]) for x in spans], [spread(grad_mix[x]) for x in spans]
    scores = [mm_nt(keys[x], wide) for x, wide in zip(spans, q_wide)]
    grad_chances = [mm_nt(vals[x], wide) for x, wide in zip(spans, g_wide)]
    chances_low, grad_scores = [], []
    for j in jets:
        masked = jnp.where(present[spans[j]] > 0.5, scores[j] * scale, -1e30)
        powers = jnp.exp(masked - jnp.max(masked, axis=0, keepdims=True))
        chances = powers * (1.0 / jnp.sum(powers, axis=0, keepdims=True))
        chances_low.append(chances.astype(LOW))
        inner = jnp.sum(chances * grad_chances[j], axis=0, keepdims=True)
        grad_scores.append((chances * (grad_chances[j] - inner) * scale).astype(LOW))
    grad_k = [mm(grad_scores[j], q_wide[j]).astype(LOW) for j in jets]
    grad_v = [mm(chances_low[j], g_wide[j]).astype(LOW) for j in jets]

    def turned(wide):
        tall = wide.T
        return jnp.concatenate([tall[h * slots : (h + 1) * slots, :] for h in range(HEADS)], axis=1)

    mixture = [mm(turned(chances_low[j]), spread(vals[spans[j]])).astype(LOW) for j in jets]
    grad_q = [mm(turned(grad_scores[j]), spread(keys[spans[j]])).astype(LOW) for j in jets]
    mixture, grad_q, grad_k, grad_v = [jnp.concatenate(x, axis=0) for x in (mixture, grad_q, grad_k, grad_v)]
    parts_ref[0] = members
    parts_ref[1] = upstream
    parts_ref[2] = mixture
    parts_ref[3] = grad_q
    parts_ref[4] = grad_k
    parts_ref[5] = grad_v
    terms(channels, bit_ref, parts_ref, send_ref, keep_ref)


def back_kernel(plan, parts_ref, wq_ref, wk_ref, wv_ref, wo_ref, *back_refs):
    count, owned = plan.chunk, plan.owned
    attended = mm(parts_ref[2], wo_ref[...]).astype(LOW)
    grad_members = mm_nt(parts_ref[3], wq_ref[...]) + mm_nt(parts_ref[4], wk_ref[...]) + mm_nt(parts_ref[5], wv_ref[...])
    grad_members = grad_members.astype(LOW)
    for w in range(plan.window):
        hot = jnp.where(plan.seat(iota((count, owned), 0), w) == iota((count, owned), 1), 1.0, 0.0).astype(LOW)
        back_refs[w][:count, :] = mm(hot, attended).astype(LOW)
        back_refs[w][count:, :] = mm(hot, grad_members).astype(LOW)


def terms(channels, bit_ref, parts_ref, send_ref, keep_ref):
    bit = bit_ref[0]
    for half, ref in ((1 - bit, send_ref), (bit, keep_ref)):
        for t in range(2):
            term = 2 * half + t
            left = parts_ref[jnp.where(term == 3, 2, 0)]
            right = parts_ref[jnp.where(term == 3, 1, 3 + term)]
            ref[t * channels : (t + 1) * channels, :] = mm_tn(left, right).astype(ref.dtype)


def return_kernel(plan, bit_ref, times_ref, *refs):
    window, count = plan.window, plan.chunk
    back_refs = refs[:window]
    place_ref, hidden_ref, cot_ref, before_ref, gathered_ref, weight_ref = refs[window : window + 6]
    out_ref, kept_ref, first_ref, last_ref, send_ref, keep_ref, rows_ref, term_ref = refs[window + 6 :]
    place = place_ref[...]
    for w in range(window):
        rows_ref[0, w * count : (w + 1) * count, :] = back_refs[w][:count, :]
        rows_ref[1, w * count : (w + 1) * count, :] = back_refs[w][count:, :]
    out_ref[...] = (hidden_ref[...].astype(FULL) + mm(place, rows_ref[0])).astype(LOW)
    grad_hidden = cot_ref[...].astype(FULL) + mm(place, rows_ref[1])
    before = before_ref[...]
    sigmoid = 1.0 / (1.0 + jnp.exp(-before))
    slope = sigmoid * (1.0 + before * (1.0 - sigmoid))
    grad_before = (grad_hidden * slope).astype(LOW)
    grad_gathered = mm_nt(grad_before, weight_ref[...]).astype(LOW).astype(FULL)

    def extended(j):
        total = None
        for b in range(plan.blocks):
            line = b * (plan.blocks + 2) + j
            part = grad_gathered[b * BLOCK : (b + 1) * BLOCK, :] * times_ref[line : line + 1, :]
            total = part if total is None else total + part
        return total.astype(LOW)

    first_ref[...] = extended(0)
    last_ref[...] = extended(plan.blocks + 1)
    for b in range(plan.blocks):
        span = slice(b * BLOCK, (b + 1) * BLOCK)
        kept_ref[span, :] = grad_hidden[span] + extended(b + 1).astype(FULL)
    half = plan.channels // 2
    term_ref[...] = mm_tn(gathered_ref[...], grad_before).reshape(2, half, plan.channels)
    send_ref[...] = term_ref[1 - bit_ref[0]].astype(LOW)
    keep_ref[...] = term_ref[bit_ref[0]]


def edges_kernel(plan, kept_ref, low_ref, high_ref, out_ref):
    last = plan.cells - BLOCK
    if last:
        out_ref[:BLOCK, :] = (kept_ref[:BLOCK, :] + low_ref[...].astype(FULL)).astype(LOW)
        if last > BLOCK:
            out_ref[BLOCK:last, :] = kept_ref[BLOCK:last, :].astype(LOW)
        out_ref[last:, :] = (kept_ref[last:, :] + high_ref[...].astype(FULL)).astype(LOW)
    else:
        out_ref[...] = (kept_ref[...] + low_ref[...].astype(FULL) + high_ref[...].astype(FULL)).astype(LOW)


def rows_of(ref, at, count):
    return ref[pl.ds(pl.multiple_of(at * count, count), count), :]


def halve_kernel(bit_ref, kept_ref, came_ref, send_ref, keep_ref):
    half = kept_ref.shape[0] // 2
    bit = bit_ref[0]
    keep_ref[...] = rows_of(kept_ref, bit, half) + rows_of(came_ref, bit, half).astype(FULL)
    send_ref[...] = (rows_of(kept_ref, 1 - bit, half) + rows_of(came_ref, 1 - bit, half).astype(FULL)).astype(LOW)


def add_kernel(*refs):
    total = refs[0][...].astype(FULL)
    for ref in refs[1:-1]:
        total = total + ref[...].astype(FULL)
    refs[-1][...] = total.astype(LOW)


def joined_kernel(bit_ref, own_ref, came_ref, term_a_ref, term_b_ref, out_ref):
    size = own_ref.shape[0]
    bit = bit_ref[0]
    out_ref[pl.ds(pl.multiple_of(bit * size, size), size), :] = own_ref[...]
    out_ref[pl.ds(pl.multiple_of((1 - bit) * size, size), size), :] = came_ref[...]
    out_ref[2 * size :, :] = (term_a_ref[...].astype(FULL) + term_b_ref[...].astype(FULL)).astype(LOW)


def total_of(squares_of):
    return jnp.sum(jnp.sum(squares_of * squares_of, axis=0, keepdims=True), axis=1, keepdims=True)


def scale_kernel(channels, bit_ref, own_ref, came_ref, *refs):
    out_refs, both_ref = refs[:5], refs[5]
    bound = math.sqrt(5.0) * channels
    squares = total_of(own_ref[...].astype(FULL)) + total_of(came_ref[...].astype(FULL))
    factor = bound / jnp.maximum(jnp.sqrt(squares), bound)
    both_ref[bit_ref[0]] = own_ref[...]
    both_ref[1 - bit_ref[0]] = came_ref[...]
    half = channels // 2
    for h in range(2):
        for t in range(2):
            out_refs[1 + 2 * h + t][...] = both_ref[h, t * channels : (t + 1) * channels, :].astype(FULL) * factor
        out_refs[0][h * half : (h + 1) * half, :] = both_ref[h, 2 * channels :, :].astype(FULL) * factor


def on_device(cell_feats, neighbours, member_cell, member_jet, cotangent, message_weight, query_weight, key_weight, value_weight, output_weight):
    events, per_device, channels = cell_feats.shape
    assert events == 1
    members_dev = member_cell.shape[1]
    plan = Plan(lax.axis_size("phi"), per_device, members_dev, channels)
    window, chunk = plan.window, plan.chunk
    place = lax.axis_index("phi").astype(jnp.int32).reshape(1)
    cells, cot, nbrs = cell_feats[0], cotangent[0], neighbours[0]
    low = shifted(cells[per_device - BLOCK :], "phi", 1)
    high = shifted(cells[:BLOCK], "phi", -1)
    total = window * chunk
    lines = -(-plan.blocks * (plan.blocks + 2) // 8) * 8
    pick, put, times, *cot_chunks = call(
        lambda *refs: index_kernel(plan, *refs),
        [((total, per_device), LOW), ((per_device, total), LOW), ((lines, channels), FULL)]
        + [((chunk, channels), LOW)] * window,
        [place, nbrs],
        [member_cell.reshape(1, members_dev), member_jet.reshape(1, members_dev), cot],
        micros=0.5,
    )
    gathered, before, hidden, *chunks = call(
        lambda *refs: hidden_kernel(plan, *refs),
        [((per_device, channels), LOW), ((per_device, channels), FULL), ((per_device, channels), LOW)]
        + [((2 * chunk, channels), LOW)] * window,
        [],
        [times, cells, low, high, message_weight, pick, *cot_chunks],
        micros=1.0,
    )

    chunks = plan.routed(chunks)
    weights = [query_weight, key_weight, value_weight, output_weight]
    core, across = [((lax.axis_index("ev") >> b) & 1).astype(jnp.int32).reshape(1) for b in range(2)]
    parts, a_send, a_keep = call(
        lambda *refs: attend_kernel(plan, *refs),
        [((6, plan.owned, channels), LOW), ((2 * channels, channels), LOW), ((2 * channels, channels), FULL)],
        [core],
        [*chunks, *weights],
        micros=2.5,
    )
    backs = call(
        lambda *refs: back_kernel(plan, *refs),
        [((2 * chunk, channels), LOW)] * window,
        [],
        [parts, *weights],
        micros=0.7,
    )
    a_came = swapped(a_send, "ev", 1)
    a_came = lax.optimization_barrier((a_came, *backs))[0]
    backs = plan.routed(backs, back=True)
    a_send, a_keep = call(halve_kernel, [((channels, channels), LOW), ((channels, channels), FULL)], [across], [a_keep, a_came])
    a_came = swapped(a_send, "ev", 2)
    half = channels // 2
    out_cells, kept, first, last, m_send, m_keep = call(
        lambda *refs: return_kernel(plan, *refs),
        [
            ((per_device, channels), LOW),
            ((per_device, channels), FULL),
            ((BLOCK, channels), LOW),
            ((BLOCK, channels), LOW),
            ((half, channels), LOW),
            ((half, channels), FULL),
        ],
        [core],
        [times, *backs, put, hidden, cot, before, gathered, message_weight],
        [pltpu.VMEM((2, total, channels), LOW), pltpu.VMEM((2, half, channels), FULL)],
        micros=4.0,
    )
    def added(rows, *parts):
        return call(add_kernel, [((rows, channels), LOW)], [], list(parts))[0]

    m_came = swapped(m_send, "ev", 1)
    a_own = added(channels, a_keep, a_came)
    from_lower = shifted(last, "phi", 1)
    from_upper = shifted(first, "phi", -1)
    m_own = added(half, m_keep, m_came)
    m_came = swapped(m_own, "ev", 2)
    masks = [1 << bit for bit in range(plan.sectors.bit_length() - 1)]
    for m_mask, a_mask in zip(masks[::-1], masks[::-1]):
        a_came = swapped(a_own, "phi", a_mask)
        m_own = added(half, m_own, m_came)
        m_came = swapped(m_own, "phi", m_mask)
        a_own = added(channels, a_own, a_came)
    a_own = lax.optimization_barrier((a_own, from_lower, from_upper))[0]
    a_came = swapped(a_own, "ev", 2)
    (grad_cells,) = call(
        lambda *refs: edges_kernel(plan, *refs), [((per_device, channels), LOW)], [], [kept, from_lower, from_upper]
    )
    m_came, grad_cells = lax.optimization_barrier((m_came, grad_cells))
    (own,) = call(joined_kernel, [((2 * channels + half, channels), LOW)], [across], [a_own, a_came, m_own, m_came])
    came = swapped(own, "ev", 1)
    grads = call(
        lambda *refs: scale_kernel(channels, *refs),
        [((channels, channels), FULL)] * 5,
        [core],
        [own, came],
        [pltpu.VMEM((2, 2 * channels + half, channels), LOW)],
        final=True,
    )
    return (out_cells[None], grad_cells[None], *grads)


def solution(mesh):
    cells = P(("groups", "ev"), "phi", None)
    flat = P(("groups", "ev"), "phi")
    weights = P("groups", None)
    return jax.shard_map(
        on_device,
        mesh=mesh,
        in_specs=(cells, cells, flat, cells, cells, P(), P(), P(), P(), P()),
        out_specs=(cells, cells, weights, weights, weights, weights, weights),
        check_vma=False,
    )
```
